768 devices in a mesh: gx: 48 (over y_lo, z, core), gy: 16 (over x, y_hi).
Axes of the slice: x: 4, y: 8 (y_hi: 4, y_lo: 2; y = y_hi * 2 + y_lo), z: 12, core: 2. Of those that a mesh axis runs over, the one named last changes fastest.
Arguments:
- pressure: float32 [192, 512, 384], P('gx', 'gy'), may hold values from -6 to 6
- previous: float32 [192, 512, 384], P('gx', 'gy'), may hold values from -6 to 6
- material: int32 [192, 512, 384], P('gx', 'gy'), may hold values from 0 to 2
- slot_cell: int32 [49152], P(('gx', 'gy')), may hold values from -1 to 49150, as said below
- angles: float32 [2, 4096], replicated, may hold values from -3.140625 to 3.140625
- spectra_in: float32 [2, 384, 4096], P(None, 'gx', 'gy'), may hold values from -6 to 6
Outputs:
- pressure_out: float32 [192, 512, 384], P('gx', 'gy')
- previous_out: float32 [192, 512, 384], P('gx', 'gy')
- spectra: float32 [2, 384, 4096], P(None, 'gx', 'gy')
The draws below stay inside these ranges and needn't reach their ends.
Inputs may be any that keep to these rules, and one draw needn't show every extreme that they name: `slot_cell`: slots j of block i = j // 64 belong to device i in the order of gx+gy. A live entry is the index (x * 32 + y) * 384 + z of a cell of that device's tile with z < 383; -1 marks an empty slot. A device's live slots come first; the number of live slots differs from device to device.
All inputs are finite; a program needn't handle non-finite values.
Results may differ from the reference program's by a relative error of at most 0.0003.
Values sent between devices are 32-bit elements; how exact they have to be, the bound alone decides.
No kernel may reach another device: no remote copies, remote signals or barrier semaphores. Data moves between devices by JAX's collectives and lax.ppermute only.
A program may use at most 32 MiB of HBM per device.

```python
import jax
import jax.numpy as jnp
from jax import lax

CX = 4
CY = 32
NZ = 384
STEPS = 16
SLOTS = 64
OBS = 4096
START = 3000
NX = 192
NY = 512
F = 384
SAMPLES = 49152
N_GY = 16


def draw_slot_cell(key, part):
    device_count = SAMPLES // SLOTS
    key_x, key_y, key_z, key_live = jax.random.split(key, 4)
    shape_two = (device_count, SLOTS)
    x_cells = jax.random.randint(key_x, shape_two, 0, CX)
    y_cells = jax.random.randint(key_y, shape_two, 0, CY)
    z_cells = jax.random.randint(key_z, shape_two, 0, NZ - 1)
    cell_ids = (x_cells * CY + y_cells) * NZ + z_cells
    live_count = jax.random.randint(key_live, (device_count, 1), 0, SLOTS + 1)
    device_ids = jnp.arange(device_count, dtype=jnp.int32)[:, None]
    live_count = jnp.where(device_ids == 0, SLOTS, live_count)
    live_count = jnp.where(device_ids == device_count - 1, jnp.minimum(live_count, SLOTS - 1), live_count)
    slot_ids = jnp.arange(SLOTS, dtype=jnp.int32)[None, :]
    last_cell = CX * CY * NZ - 2
    cell_ids = jnp.where((device_ids == 0) & (slot_ids == 0), last_cell, cell_ids)
    chosen = jnp.where(slot_ids < live_count, cell_ids, -1)
    return chosen.reshape(-1).astype(jnp.int32)


def place_ends(drawn, rng, smallest, top_value):
    place = [jax.random.randint(jax.random.fold_in(rng, axis), (), 0, length) for axis, length in enumerate(drawn.shape)]
    longest = drawn.shape.index(max(drawn.shape))
    next_to = place[:longest] + [(place[longest] + 1) % drawn.shape[longest]] + place[longest + 1:]
    return drawn.at[tuple(place)].set(smallest).at[tuple(next_to)].set(top_value)


def shard_levels(stream_key, extent, cuts, least, top_value):
    level, own = 1.0, jax.random.fold_in(stream_key, 6)
    for dim, blocks in cuts:
        heights = jnp.exp(jax.random.uniform(jax.random.fold_in(own, dim), (blocks,), jnp.float32, least / len(cuts), top_value / len(cuts)))
        level = level * jnp.repeat(heights, extent[dim] // blocks).reshape([-1 if axis == dim else 1 for axis in range(len(extent))])
    return level


def bell_draw(key, shape, width, bound, pieces=(), kind=jnp.bfloat16):
    level = shard_levels(key, shape, pieces, -0.22, 0.18) if pieces else 1.0
    drawn = jax.random.normal(key, shape, jnp.float32) * width * level
    return jnp.minimum(jnp.maximum(drawn, -bound), bound).astype(kind)


def setup_inputs(seed: int = 0) -> dict:
    splits = jax.random.split(jax.random.key(seed), 7)
    pressure = bell_draw(splits[0], (NX, NY, NZ), 1.0, 6.0, ((0, 48), (1, 16)), jnp.float32)
    previous = bell_draw(splits[1], (NX, NY, NZ), 1.0, 6.0, ((0, 48), (1, 16)), jnp.float32)
    material = place_ends(jax.random.randint(splits[2], (NX, NY, NZ), 0, 3), jax.random.fold_in(splits[2], 1), 0, 2).astype(jnp.int32)
    slot_cell = draw_slot_cell(jax.random.fold_in(splits[6], 71), 0)
    angles = jnp.clip(jax.random.uniform(splits[4], (2, OBS), jnp.float32, -3.140625, 3.140625), -3.140625, 3.140625)
    spectra_in = bell_draw(splits[5], (2, F, OBS), 1.0, 6.0, ((1, 48), (2, 16)), jnp.float32)
    return dict(pressure=pressure, previous=previous, material=material, slot_cell=slot_cell, angles=angles, spectra_in=spectra_in)


SIGMA_ABS = 0.5
LAMBDA_SQ = 0.25
KAPPA = 0.37

def advance(padded, open_big, before, loss):
    center = padded[1:-1, 1:-1]
    open_center = open_big[1:-1, 1:-1]
    summed = open_big[:-2, 1:-1] * (padded[:-2, 1:-1] - center)
    summed = summed + open_big[2:, 1:-1] * (padded[2:, 1:-1] - center)
    summed = summed + open_big[1:-1, :-2] * (padded[1:-1, :-2] - center)
    summed = summed + open_big[1:-1, 2:] * (padded[1:-1, 2:] - center)
    z_pad = ((0, 0), (0, 0), (1, 1))
    center_z = jnp.pad(center, z_pad)
    open_z = jnp.pad(open_center, z_pad)
    summed = summed + open_z[:, :, 2:] * (center_z[:, :, 2:] - center)
    summed = summed + open_z[:, :, :-2] * (center_z[:, :, :-2] - center)
    update = 2.0 * center - (1.0 - loss) * before + LAMBDA_SQ * (open_center * summed)
    return open_center * update / (1.0 + loss)

def project(angle_rows, coords, series_g, series_p):
    elevation = angle_rows[0]
    azimuth = angle_rows[1]
    unit_x = jnp.cos(elevation) * jnp.cos(azimuth)
    unit_y = jnp.cos(elevation) * jnp.sin(azimuth)
    unit_z = jnp.sin(elevation)
    phases = KAPPA * (unit_x[:, None] * coords[0][None, :] + unit_y[:, None] * coords[1][None, :] + unit_z[:, None] * coords[2][None, :])
    best_prec = lax.Precision.HIGHEST
    normal_part = jnp.einsum('os,ts->ot', jnp.cos(phases), series_g, precision=best_prec)
    pressure_part = jnp.einsum('os,ts->ot', unit_z[:, None] * jnp.sin(phases), series_p, precision=best_prec)
    return normal_part + pressure_part

def reference(pressure, previous, material, slot_cell, angles, spectra_in):
    open_cell = (material != 1).astype(jnp.float32)
    loss = jnp.where(material == 2, jnp.float32(SIGMA_ABS), jnp.float32(0.0))
    xy_pad = ((1, 1), (1, 1), (0, 0))
    open_big = jnp.pad(open_cell, xy_pad)
    slot_ids = jnp.arange(SAMPLES, dtype=jnp.int32)
    device_ids = slot_ids // SLOTS
    safe_cell = jnp.maximum(slot_cell, 0).astype(jnp.int32)
    x_global = device_ids // N_GY * CX + safe_cell // (CY * NZ)
    y_global = device_ids % N_GY * CY + safe_cell // NZ % CY
    z_global = safe_cell % NZ
    live_slot = (slot_cell >= 0).astype(jnp.float32)
    current = pressure
    before = previous
    rows_g = []
    rows_p = []
    for step_now in range(STEPS):
        following = advance(jnp.pad(current, xy_pad), open_big, before, loss)
        before = current
        current = following
        cell_value = current[x_global, y_global, z_global]
        above_value = current[x_global, y_global, z_global + 1]
        rows_p.append(live_slot * cell_value)
        rows_g.append(live_slot * (above_value - cell_value))
    series_g = jnp.stack(rows_g)
    series_p = jnp.stack(rows_p)
    coords = jnp.stack([x_global, y_global, z_global]).astype(jnp.float32)
    device_count = SAMPLES // SLOTS
    blocks_g = series_g.reshape(STEPS, device_count, SLOTS).transpose(1, 0, 2)
    blocks_p = series_p.reshape(STEPS, device_count, SLOTS).transpose(1, 0, 2)
    blocks_c = coords.reshape(3, device_count, SLOTS).transpose(1, 0, 2)

    def accumulate(running, sample_block):
        block_g, block_p, block_c = sample_block
        return (running + project(angles, block_c, block_g, block_p), None)
    traces, unused = lax.scan(accumulate, jnp.zeros((OBS, STEPS), jnp.float32), (blocks_g, blocks_p, blocks_c))
    traces = traces / jnp.sqrt(jnp.float32(SAMPLES))
    bin_ids = jnp.arange(F, dtype=jnp.int32)
    time_ids = jnp.arange(STEPS, dtype=jnp.int32)
    turn_ids = (START + time_ids)[None, :] * (bin_ids + 1)[:, None] % (2 * (F + 1))
    angles_kt = jnp.pi * turn_ids.astype(jnp.float32) / (F + 1)
    best_prec = lax.Precision.HIGHEST
    real_part = spectra_in[0] + jnp.dot(jnp.cos(angles_kt), traces.T, precision=best_prec)
    imag_part = spectra_in[1] - jnp.dot(jnp.sin(angles_kt), traces.T, precision=best_prec)
    return (current, before, jnp.stack([real_part, imag_part]))
```

```python
import jax
import jax.numpy as jnp
from jax import lax
from jax.experimental import pallas as pl
from jax.experimental.pallas import tpu as pltpu
from jax.sharding import PartitionSpec as P

STEPS = 16
START = 3000
KAPPA = 0.37
W = 4
F32 = jnp.float32
TURN = 6.283185307179586


def call(kernel, outs, scratch=(), name=None):
    return pl.pallas_call(
        kernel,
        out_shape=outs,
        scratch_shapes=list(scratch),
        compiler_params=pltpu.CompilerParams(vmem_limit_bytes=48 * 1024 * 1024),
        name=name,
    )


def low_half(shape):
    return lax.broadcasted_iota(jnp.int32, shape, len(shape) - 2) % 8 < 4


def edge_tiles(cur, bef):
    first, last = (cur[:, 0:8], bef[:, 0:8]), (cur[:, -8:], bef[:, -8:])
    keep = low_half(first[0].shape)
    down = jnp.where(keep, first[0], pltpu.roll(first[1], 4, 1))
    up = jnp.where(keep, pltpu.roll(last[1], 4, 1), last[0])
    return up, down


def prepare_kernel(cur_ref, bef_ref, mat_ref, state_ref, up_ref, down_ref):
    tx = cur_ref.shape[0]
    mat = mat_ref[...]
    gain = jnp.where(mat == 1, 0.0, jnp.where(mat == 2, F32(1.0) / F32(1.5), F32(1.0)))
    cur = jnp.where(mat == 1, 0.0, cur_ref[...])
    bef = jnp.where(mat == 1, 0.0, bef_ref[...])
    state_ref[0:tx] = cur
    state_ref[tx : 2 * tx] = bef
    state_ref[2 * tx :] = gain
    up, down = edge_tiles(cur, bef)
    up_ref[0:tx] = up
    up_ref[tx:] = gain[:, -8:]
    down_ref[0:tx] = down
    down_ref[tx:] = gain[:, 0:8]


def shifted(v, axis, by, edge):
    n = v.shape[axis]
    moved = pltpu.roll(v, by % n, axis)
    if not edge:
        return moved
    ids = lax.broadcasted_iota(jnp.int32, v.shape, axis)
    return jnp.where(ids == (0 if by == 1 else n - 1), 0.0, moved)


def neighbours(plane, x):
    v = plane(x)
    total = plane(x - 1) + plane(x + 1)
    total = total + (shifted(v, 0, 1, False) + shifted(v, 0, -1, False))
    return v, total + (shifted(v, 1, 1, True) + shifted(v, 1, -1, True))


def window_kernel(first, final, tx, ty, *refs):
    refs = list(refs)
    own, xlo, xhi = refs[:3]
    columns = (refs[3:6], refs[6:9])
    refs = refs[9:]
    if not first:
        gain_in, count_in = refs[:2]
        refs = refs[2:]
    cell_col, cell_row = refs[:2]
    refs = refs[2:]
    if final:
        out_cur, out_bef, sample_ref, one, two = refs
    elif first:
        state_ref, up_ref, down_ref, sample_ref, gain_out, count_out, one, two = refs
    else:
        state_ref, up_ref, down_ref, sample_ref, one, two = refs
    gain_ref, count_ref = (gain_out, count_out) if first else (gain_in, count_in)
    keep = low_half((tx, 8, own.shape[2]))
    for part, tiles in enumerate((xlo, own, xhi)):
        rows = slice(part * tx, (part + 1) * tx)
        lower, upper = columns[0][part], columns[1][part]
        one[rows, 0:ty] = tiles[0:tx]
        two[rows, 0:ty] = tiles[tx : 2 * tx]
        one[rows, ty:] = jnp.where(keep, upper[0:tx], lower[0:tx])
        two[rows, ty:] = pltpu.roll(jnp.where(keep, lower[0:tx], upper[0:tx]), 4, 1)
        if first:
            gain_ref[rows, 0:ty] = tiles[2 * tx :]
            gain_ref[rows, ty:] = jnp.where(keep, upper[tx:], lower[tx:])
    if first:
        count_ref[...] = jnp.zeros(count_ref.shape, F32)
        for x in range(1, 3 * tx - 1):
            opened = lambda i: jnp.where(gain_ref[i] > 0.0, F32(1.0), F32(0.0))
            count_ref[x] = neighbours(opened, x)[1]
    nz = own.shape[2]
    cell = cell_row[...]
    live = cell >= 0
    safe = jnp.maximum(cell, 0)
    lane = lax.broadcasted_iota(jnp.int32, (1, 128), 1)
    z_of = safe % nz + (lane >= 64).astype(jnp.int32)
    row_of = jnp.where(live, safe // nz, -1)
    zhot = (lax.broadcasted_iota(jnp.int32, (nz, 128), 0) == z_of).astype(jnp.bfloat16)
    rhot = lax.broadcasted_iota(jnp.int32, (tx * ty, 128), 0) == row_of

    for step in range(1, W + 1):
        cur, bef = (one, two) if step % 2 else (two, one)
        for x in range(step, 3 * tx - step):
            v, total = neighbours(lambda i: cur[i], x)
            b = bef[x]
            inner = 0.25 * (total - count_ref[x] * v) + 2.0 * (v - b)
            bef[x] = gain_ref[x] * inner + b
        now = bef[tx : 2 * tx, 0:ty].reshape(tx * ty, nz)
        high = now.astype(jnp.bfloat16)
        low = (now - high.astype(F32)).astype(jnp.bfloat16)
        dot = lambda a: jnp.dot(a, zhot, preferred_element_type=F32)
        picked = jnp.where(rhot, dot(high) + dot(low), 0.0)
        sample_ref[pl.ds(step - 1, 1), :] = jnp.sum(picked, axis=0, keepdims=True)
    cur, bef = (one, two) if W % 2 == 0 else (two, one)
    cur, bef = cur[tx : 2 * tx, 0:ty], bef[tx : 2 * tx, 0:ty]
    if final:
        out_cur[...] = cur
        out_bef[...] = bef
    else:
        state_ref[0:tx] = cur
        state_ref[tx:] = bef
        up, down = edge_tiles(cur, bef)
        up_ref[...] = up
        down_ref[...] = down


def sin_cos_turns(p):
    r = p - jnp.floor(p + 0.5)
    q = r * r
    s = F32(-0.00702838626472677)
    for c in (0.0820504017189708, -0.599252197803835, 2.55016331894515, -5.16771276462447, 3.14159265353629):
        s = s * q + F32(c)
    s = s * r
    c_ = F32(-0.0243963243010939)
    for c in (0.234937313786045, -1.33521200304381, 4.0587091595557, -4.93480213707881, 0.999999999779904):
        c_ = c_ * q + F32(c)
    return 2.0 * s * c_, 1.0 - 2.0 * s * s


def phase_kernel(coord_ref, angle_ref, high_ref, low_ref):
    ux, uy, uz = angle_ref[0:1], angle_ref[1:2], angle_ref[2:3]
    slots = 64
    for d in range(coord_ref.shape[0] // slots):
        rows = pl.ds(d * slots, slots)
        xyz = coord_ref[rows, :]
        turns = (KAPPA / TURN) * (ux * xyz[:, 0:1] + uy * xyz[:, 1:2] + uz * xyz[:, 2:3])
        s, c = sin_cos_turns(turns)
        for k, v in enumerate((uz * s - c, c)):
            high = v.astype(jnp.bfloat16)
            at = pl.ds((2 * d + k) * slots, slots)
            high_ref[at, :] = high
            low_ref[at, :] = (v - high.astype(F32)).astype(jnp.bfloat16)


def project_kernel(sample_ref, high_ref, low_ref, out_ref):
    total = jnp.zeros(out_ref.shape, F32)
    for d in range(sample_ref.shape[0]):
        s = sample_ref[d]
        rows = slice(d * 128, (d + 1) * 128)
        high = s.astype(jnp.bfloat16)
        low = (s - high.astype(F32)).astype(jnp.bfloat16)
        dot = lambda a, b: jnp.dot(a, b, preferred_element_type=F32)
        total = total + dot(high, high_ref[rows]) + (dot(low, high_ref[rows]) + dot(high, low_ref[rows]))
    out_ref[...] = total


def spectra_kernel(scale, trace_ref, wave_ref, spec_ref, out_ref):
    dot = lambda a, b: jnp.dot(a, b, preferred_element_type=F32, precision=lax.Precision.HIGHEST)
    traces = trace_ref[...] * F32(scale)
    out_ref[0] = spec_ref[0] + dot(wave_ref[0], traces)
    out_ref[1] = spec_ref[1] - dot(wave_ref[1], traces)


def steps_of(count, by):
    return [(i, i + by) for i in range(count) if 0 <= i + by < count]


def sum_gx(v):
    return lax.psum(v, "gx")


def body(pressure, previous, material, slot_cell, angles, spectra_in):
    tx, ty, nz = pressure.shape
    ngx, ngy = lax.axis_size("gx"), lax.axis_size("gy")
    gx, gy = lax.axis_index("gx"), lax.axis_index("gy")
    shape = lambda *s: jax.ShapeDtypeStruct(s, F32)

    def corner(v, dx, dy):
        pairs = [
            (i * ngy + j, (i + dx) * ngy + j + dy)
            for i in range(ngx)
            for j in range(ngy)
            if 0 <= i + dx < ngx and 0 <= j + dy < ngy
        ]
        return lax.ppermute(v, ("gx", "gy"), pairs)

    def exchange(state, up, down):
        xlo = lax.ppermute(state, "gx", steps_of(ngx, 1))
        xhi = lax.ppermute(state, "gx", steps_of(ngx, -1))
        lower = [corner(up, dx, 1) for dx in (1, 0, -1)]
        upper = [corner(down, dx, -1) for dx in (1, 0, -1)]
        return [state, xlo, xhi, *lower, *upper]

    cells = jnp.concatenate([slot_cell, slot_cell])[None, :]
    state, up, down = call(
        prepare_kernel, [shape(3 * tx, ty, nz), shape(2 * tx, 8, nz), shape(2 * tx, 8, nz)], name="prepare"
    )(pressure, previous, material)
    big = (3 * tx, ty + 8, nz)
    scratch = [pltpu.VMEM(big, F32), pltpu.VMEM(big, F32)]
    rounds = STEPS // W
    samples, extra = [], []
    for r in range(rounds):
        first, final = r == 0, r == rounds - 1
        outs = [shape(tx, ty, nz)] * 2 if final else [shape(2 * tx, ty, nz), shape(tx, 8, nz), shape(tx, 8, nz)]
        outs = outs + [shape(W, 128)] + ([shape(*big)] * 2 if first else [])
        kernel = lambda *refs, first=first, final=final: window_kernel(first, final, tx, ty, *refs)
        got = call(kernel, outs, scratch, name=f"window{r}")(*exchange(state, up, down), *extra, cells.T, cells)
        if final:
            current, before, sample = got
        elif first:
            state, up, down, sample, *extra = got
        else:
            state, up, down, sample = got
        samples.append(sample)

    row_cells = jnp.maximum(lax.all_gather(slot_cell, "gy"), 0)
    x_at = gx * tx + row_cells // (ty * nz)
    y_at = jnp.arange(ngy, dtype=jnp.int32)[:, None] * ty + row_cells // nz % ty
    coords = jnp.stack([x_at, y_at, row_cells % nz], axis=-1).astype(F32).reshape(-1, 3)
    own = spectra_in.shape[2]
    elevation, azimuth = lax.dynamic_slice_in_dim(angles, gy * own, own, axis=1)
    units = jnp.stack(
        [jnp.cos(elevation) * jnp.cos(azimuth), jnp.cos(elevation) * jnp.sin(azimuth), jnp.sin(elevation)]
    )
    depth = coords.shape[0] * 2
    half = jax.ShapeDtypeStruct((depth, own), jnp.bfloat16)
    high, low = call(phase_kernel, [half, half], name="phases")(coords, units)

    series = lax.all_gather(jnp.concatenate(samples), "gy")
    part = call(project_kernel, shape(STEPS, own), name="project")(series, high, low)
    traces = sum_gx(part)

    bin_local = spectra_in.shape[1]
    bin_total = bin_local * ngx
    bin_ids = gx * bin_local + jnp.arange(bin_local, dtype=jnp.int32)
    time_ids = jnp.arange(STEPS, dtype=jnp.int32)
    turn_ids = (START + time_ids)[None, :] * (bin_ids + 1)[:, None] % (2 * (bin_total + 1))
    theta = jnp.pi * turn_ids.astype(F32) / (bin_total + 1)
    waves = jnp.stack([jnp.cos(theta), jnp.sin(theta)])
    scale = float(slot_cell.shape[0] * ngx * ngy) ** -0.5
    spectra = call(
        lambda *refs: spectra_kernel(scale, *refs), shape(*spectra_in.shape), name="spectra"
    )(traces, waves, spectra_in)
    return current, before, spectra


def solution(mesh):
    return jax.shard_map(
        body,
        mesh=mesh,
        in_specs=(
            P("gx", "gy", None),
            P("gx", "gy", None),
            P("gx", "gy", None),
            P(("gx", "gy")),
            P(),
            P(None, "gx", "gy"),
        ),
        out_specs=(P("gx", "gy", None), P("gx", "gy", None), P(None, "gx", "gy")),
        check_vma=False,
    )
```

```python
import jax
import jax.numpy as jnp
from jax import lax
from jax.experimental import pallas as pl
from jax.experimental.pallas import tpu as pltpu
from jax.sharding import PartitionSpec as P

STEPS = 16
START = 3000
KAPPA = 0.37
W = 4
Y = 8
F32 = jnp.float32
BF16 = jnp.bfloat16
TURN = 6.283185307179586


def call(kernel, outs, scratch=(), name=None):
    return pl.pallas_call(
        kernel,
        out_shape=outs,
        scratch_shapes=list(scratch),
        compiler_params=pltpu.CompilerParams(vmem_limit_bytes=48 * 1024 * 1024),
        name=name,
    )


def edges(ref, ty):
    even = lax.axis_index("gy") % 2 == 0
    top, bottom = ty - Y, 0
    at = lambda row: ref[:, pl.ds(pl.multiple_of(row, 8), Y)]
    return at(jnp.where(even, top, bottom)), at(jnp.where(even, bottom, top))


def prepare_kernel(cur_ref, bef_ref, mat_ref, state_ref, a_ref, b_ref):
    tx, ty, _ = cur_ref.shape
    mat = mat_ref[...]
    state_ref[0:tx] = jnp.where(mat == 1, 0.0, cur_ref[...])
    state_ref[tx : 2 * tx] = jnp.where(mat == 1, 0.0, bef_ref[...])
    state_ref[2 * tx :] = jnp.where(mat == 1, 0.0, jnp.where(mat == 2, F32(1.0) / F32(1.5), F32(1.0)))
    a_ref[...], b_ref[...] = edges(state_ref, ty)


def shifted(v, axis, by, edge):
    n = v.shape[axis]
    moved = pltpu.roll(v, by % n, axis)
    if not edge:
        return moved
    ids = lax.broadcasted_iota(jnp.int32, v.shape, axis)
    return jnp.where(ids == (0 if by == 1 else n - 1), 0.0, moved)


def neighbours(plane, x):
    v = plane(x)
    total = plane(x - 1) + plane(x + 1)
    total = total + (shifted(v, 0, 1, False) + shifted(v, 0, -1, False))
    return v, total + (shifted(v, 1, 1, True) + shifted(v, 1, -1, True))


def narrow(v, ty):
    above, below = v[..., ty : ty + 8, :], v[..., ty + 8 :, :]
    low = lax.broadcasted_iota(jnp.int32, above.shape, above.ndim - 2) < 4
    return jnp.concatenate([v[..., 0:ty, :], jnp.where(low, above, below)], axis=-2)


def window_kernel(kind, tx, ty, *refs):
    refs = list(refs)
    take = lambda n: [refs.pop(0) for _ in range(n)]
    own, x_a, x_b = take(3)
    (cell_row,) = take(1)
    if kind != "first":
        gain_ref, count_ref = take(2)
    done = take(3) if kind == "last" else ()
    if kind == "last":
        out_cur, out_bef, series_ref = take(3)
    else:
        state_ref, *rest = take({"first": 1, "inner": 3, "wide": 1}[kind])
        (sample_ref,) = take(1)
    if kind == "first":
        gain_ref, count_ref, gain4_ref, count4_ref = take(4)
    one, two = take(2)
    nz = own.shape[2]
    odd = lax.axis_index("gx") % 2
    at_a = (1 - odd) * 2 * tx
    at_b = odd * 2 * tx
    for at, tiles in ((tx, own), (at_a, x_a), (at_b, x_b)):
        one[pl.ds(at, tx)] = tiles[0:tx]
        two[pl.ds(at, tx)] = tiles[tx : 2 * tx]
        if kind == "first":
            gain_ref[pl.ds(at, tx)] = tiles[2 * tx :]
    if kind == "first":
        count_ref[...] = jnp.zeros(count_ref.shape, F32)
        opened = lambda i: jnp.where(gain_ref[i] > 0.0, F32(1.0), F32(0.0))
        for x in range(1, 3 * tx - 1):
            count_ref[x] = neighbours(opened, x)[1]
        gain4_ref[...] = narrow(gain_ref[...], ty)
        count4_ref[...] = narrow(count_ref[...], ty)
    cell = cell_row[...]
    safe = jnp.maximum(cell, 0)
    lane = lax.broadcasted_iota(jnp.int32, (1, 128), 1)
    z_of = safe % nz + (lane >= 64).astype(jnp.int32)
    row_of = jnp.where(cell >= 0, safe // nz, -1)
    zhot = (lax.broadcasted_iota(jnp.int32, (nz, 128), 0) == z_of).astype(BF16)
    rhot = lax.broadcasted_iota(jnp.int32, (tx * ty, 128), 0) == row_of

    picks = []
    for step in range(1, W + 1):
        cur, bef = (one, two) if step % 2 else (two, one)
        for x in range(step, 3 * tx - step):
            v, total = neighbours(lambda i: cur[i], x)
            b = bef[x]
            inner = 0.25 * (total - count_ref[x] * v) + 2.0 * (v - b)
            bef[x] = gain_ref[x] * inner + b
        now = bef[tx : 2 * tx, 0:ty].reshape(tx * ty, nz)
        high = now.astype(BF16)
        low = (now - high.astype(F32)).astype(BF16)
        dot = lambda a: jnp.dot(a, zhot, preferred_element_type=F32)
        picked = jnp.where(rhot, dot(high) + dot(low), 0.0)
        picks.append(jnp.sum(picked, axis=0, keepdims=True))
    cur, bef = (one, two) if W % 2 == 0 else (two, one)
    cur, bef = cur.at[tx : 2 * tx], bef.at[tx : 2 * tx]
    if kind == "last":
        out_cur[...] = cur[:, 0:ty]
        out_bef[...] = bef[:, 0:ty]
        cells = jnp.broadcast_to(cell.astype(F32), (8, 128))
        series = jnp.concatenate([*(d[...] for d in done), *picks, cells])
        for d in range(series_ref.shape[0]):
            series_ref[d] = series
        return
    for k, pick in enumerate(picks):
        sample_ref[pl.ds(k, 1), :] = pick
    if kind == "inner":
        state_ref[0:tx] = cur[:, 0:ty]
        state_ref[tx:] = bef[:, 0:ty]
        rest[0][...], rest[1][...] = edges(state_ref, ty)
    else:
        state_ref[0:tx] = narrow(cur[...], ty)
        state_ref[tx:] = narrow(bef[...], ty)


def sin_cos_turns(p):
    r = p - jnp.floor(p + 0.5)
    q = r * r
    s = F32(-0.00702838626472677)
    for k in (0.0820504017189708, -0.599252197803835, 2.55016331894515, -5.16771276462447, 3.14159265353629):
        s = s * q + F32(k)
    s = s * r
    c = F32(-0.0243963243010939)
    for k in (0.234937313786045, -1.33521200304381, 4.0587091595557, -4.93480213707881, 0.999999999779904):
        c = c * q + F32(k)
    return 2.0 * s * c, 1.0 - 2.0 * s * s


def project_kernel(tx, ty, nz, own, series_ref, angle_ref, out_ref):
    slots = 64
    ndev, _, lanes = series_ref.shape
    at = pl.multiple_of(lax.axis_index("gy") * own, 128)
    sin_e, cos_e = sin_cos_turns(angle_ref[0:1, pl.ds(at, own)] * (1.0 / TURN))
    sin_a, cos_a = sin_cos_turns(angle_ref[1:2, pl.ds(at, own)] * (1.0 / TURN))
    ux, uy, uz = cos_e * cos_a, cos_e * sin_a, sin_e
    rows = [series_ref[d, STEPS : STEPS + 1, :] for d in range(ndev)]
    cells = jnp.concatenate([*rows, jnp.zeros((lanes - ndev, lanes), F32)]).T[0:slots]
    cells = jnp.maximum(cells, 0.0).astype(jnp.int32)
    device = lax.broadcasted_iota(jnp.int32, cells.shape, 1)
    x_of = (lax.axis_index("gx") * tx + cells // (ty * nz)).astype(F32)
    y_of = (device * ty + cells // nz % ty).astype(F32)
    z_of = (cells % nz).astype(F32)
    total = jnp.zeros((STEPS, own), F32)
    for d in range(ndev):
        column = lambda v: v[:, d : d + 1]
        turns = (KAPPA / TURN) * (ux * column(x_of) + uy * column(y_of) + uz * column(z_of))
        s, c = sin_cos_turns(turns)
        waves = jnp.concatenate([uz * s - c, c])
        wave_high = waves.astype(BF16)
        wave_low = (waves - wave_high.astype(F32)).astype(BF16)
        v = series_ref[d, 0:STEPS, :]
        high = v.astype(BF16)
        low = (v - high.astype(F32)).astype(BF16)
        dot = lambda a, b: jnp.dot(a, b, preferred_element_type=F32)
        total = total + dot(high, wave_high) + (dot(low, wave_high) + dot(high, wave_low))
    out_ref[...] = jnp.zeros(out_ref.shape, F32)
    for k in range(own // 128):
        out_ref[k * STEPS : (k + 1) * STEPS] = total[:, k * 128 : (k + 1) * 128]


def sum_kernel(part_ref, out_ref):
    total = jnp.sum(part_ref[...], axis=0, keepdims=True)
    out_ref[...] = jnp.broadcast_to(total, out_ref.shape)


def spectra_kernel(scale, bin_total, trace_ref, spec_ref, out_ref):
    bins = spec_ref.shape[1]
    period = 2 * (bin_total + 1)
    bin_of = lax.axis_index("gx") * bins + lax.broadcasted_iota(jnp.int32, (bins, STEPS), 0) + 1
    step_of = lax.broadcasted_iota(jnp.int32, (bins, STEPS), 1) + START
    turn = (step_of * bin_of).astype(F32)
    turn = turn - period * jnp.floor(turn * (1.0 / period))
    sin_t, cos_t = sin_cos_turns(turn * (1.0 / period))
    parts = [trace_ref[k * STEPS : (k + 1) * STEPS] for k in range(spec_ref.shape[2] // 128)]
    traces = jnp.concatenate(parts, axis=1) * F32(scale)
    dot = lambda a: jnp.dot(a, traces, preferred_element_type=F32, precision=lax.Precision.HIGHEST)
    out_ref[0] = spec_ref[0] + dot(cos_t)
    out_ref[1] = spec_ref[1] - dot(sin_t)


def swap(v, axis):
    count = lax.axis_size(axis)
    even_odd = [(i, i ^ 1) for i in range(count) if i ^ 1 < count]
    odd_even = [(i, ((i + 1) ^ 1) - 1) for i in range(1, count) if ((i + 1) ^ 1) - 1 < count]
    v_a, v_b = v
    got_b = lax.ppermute(v_b, axis, odd_even)
    return lax.ppermute(v_a, axis, even_odd), got_b


def body(pressure, previous, material, slot_cell, angles, spectra_in):
    tx, ty, nz = pressure.shape
    ngx, ngy = lax.axis_size("gx"), lax.axis_size("gy")
    even_y = lax.axis_index("gy") % 2 == 0
    shape = lambda *s: jax.ShapeDtypeStruct(s, F32)
    window = lambda kind: lambda *refs: window_kernel(kind, tx, ty, *refs)
    wide, thin = (3 * tx, ty + 2 * Y, nz), (3 * tx, ty + 2 * W, nz)
    scratch = lambda s: [pltpu.VMEM(s, F32)] * 2

    def exchange_y(state, a, b):
        a, b = swap((a, b), "gy")
        return jnp.concatenate([state, jnp.where(even_y, a, b), jnp.where(even_y, b, a)], axis=1)

    def exchange_x(state):
        return [state, *swap((state, state), "gx"), cells]

    cells = jnp.concatenate([slot_cell, slot_cell])[None, :]
    state, a, b = call(
        prepare_kernel, [shape(3 * tx, ty, nz), shape(3 * tx, Y, nz), shape(3 * tx, Y, nz)], name="prepare"
    )(pressure, previous, material)
    state = exchange_y(state, a, b)
    part = shape(W, 128)
    state, first, gain, count, gain4, count4 = call(
        window("first"),
        [shape(2 * tx, *thin[1:]), part, shape(*wide), shape(*wide), shape(*thin), shape(*thin)],
        scratch(wide),
        name="window_first",
    )(*exchange_x(state))
    state, a, b, second = call(
        window("inner"), [shape(2 * tx, ty, nz), shape(2 * tx, Y, nz), shape(2 * tx, Y, nz), part], scratch(thin), name="window_inner"
    )(*exchange_x(state), gain4, count4)
    state = exchange_y(state, a, b)
    state, third = call(window("wide"), [shape(2 * tx, *thin[1:]), part], scratch(wide), name="window_wide")(
        *exchange_x(state), gain, count
    )
    current, before, series = call(
        window("last"), [shape(tx, ty, nz), shape(tx, ty, nz), shape(ngy, STEPS + 8, 128)], scratch(thin), name="window_last"
    )(*exchange_x(state), gain4, count4, first, second, third)

    series = lax.all_to_all(series, "gy", 0, 0, tiled=True)
    own = spectra_in.shape[2]
    rows = pl.cdiv(STEPS * own // 128, ngx)
    partial = call(lambda *refs: project_kernel(tx, ty, nz, own, *refs), shape(ngx * rows, 128), name="project")(series, angles)
    partial = lax.all_to_all(partial, "gx", 0, 0, tiled=True).reshape(ngx, rows * 128)
    total = call(sum_kernel, shape(ngx, rows * 128), name="total")(partial)
    traces = lax.all_to_all(total.reshape(ngx * rows, 128), "gx", 0, 0, tiled=True)
    scale = float(slot_cell.shape[0] * ngx * ngy) ** -0.5
    bins = spectra_in.shape[1] * ngx
    spectra = call(lambda *refs: spectra_kernel(scale, bins, *refs), shape(*spectra_in.shape), name="spectra")(traces, spectra_in)
    return current, before, spectra


def solution(mesh):
    return jax.shard_map(
        body,
        mesh=mesh,
        in_specs=(
            P("gx", "gy", None),
            P("gx", "gy", None),
            P("gx", "gy", None),
            P(("gx", "gy")),
            P(),
            P(None, "gx", "gy"),
        ),
        out_specs=(P("gx", "gy", None), P("gx", "gy", None), P(None, "gx", "gy")),
        check_vma=False,
    )
```

```python
import jax
import jax.numpy as jnp
from jax import lax
from jax.experimental import pallas as pl
from jax.experimental.pallas import tpu as pltpu
from jax.sharding import PartitionSpec as P

STEPS = 16
START = 3000
KAPPA = 0.37
W = 4
Y = 8
F32 = jnp.float32
BF16 = jnp.bfloat16
TURN = 6.283185307179586


def call(kernel, outs, scratch=(), name=None, specs=None):
    more = {} if specs is None else {"in_specs": specs}
    return pl.pallas_call(
        kernel,
        out_shape=outs,
        scratch_shapes=list(scratch),
        compiler_params=pltpu.CompilerParams(vmem_limit_bytes=16 * 1024 * 1024),
        name=name,
        **more,
    )


def edges(ref, ty):
    even = lax.axis_index("gy") % 2 == 0
    top, bottom = ty - Y, 0
    at = lambda row: ref[:, pl.ds(pl.multiple_of(row, 8), Y)]
    return at(jnp.where(even, top, bottom)), at(jnp.where(even, bottom, top))


def prepare_kernel(cur_hbm, bef_hbm, mat_hbm, state_ref, a_ref, b_ref, cur_ref, bef_ref, mat_ref, sems):
    tx, ty, _ = cur_ref.shape
    pairs = ((mat_hbm, mat_ref), (cur_hbm, cur_ref), (bef_hbm, bef_ref))
    copies = [pltpu.make_async_copy(src, dst, sems.at[k]) for k, (src, dst) in enumerate(pairs)]
    for copy in copies:
        copy.start()
    copies[0].wait()
    mat = mat_ref[...]
    state_ref[2 * tx :] = jnp.where(mat == 1, 0.0, jnp.where(mat == 2, F32(1.0) / F32(1.5), F32(1.0)))
    copies[1].wait()
    state_ref[0:tx] = jnp.where(mat == 1, 0.0, cur_ref[...])
    copies[2].wait()
    state_ref[tx : 2 * tx] = jnp.where(mat == 1, 0.0, bef_ref[...])
    a_ref[...], b_ref[...] = edges(state_ref, ty)


def message_tiles(fields, tx, ty, reach):
    tiles = []
    for field in range(fields):
        late = 1 if field == 1 else 0
        for d in range(1, W + 1 - late):
            tiles += [(field, d, 8 * k, False) for k in range(ty // 8)]
            rows = reach - d - late
            if rows > 4:
                tiles += [(field, d, ty, False), (field, d, ty + 8, False)]
            elif rows > 0:
                tiles.append((field, d, ty, True))
    return tiles


def write_messages(own, a_ref, b_ref, fields, tx, ty, reach):
    odd = lax.axis_index("gx") % 2
    wide = own.shape[1] == ty + 16
    low = lax.broadcasted_iota(jnp.int32, (8, own.shape[2]), 0) < 4
    for k, (field, d, row, packed) in enumerate(message_tiles(fields, tx, ty, reach)):
        for ref, below in ((a_ref, odd), (b_ref, 1 - odd)):
            plane = field * tx + below * (d - 1) + (1 - below) * (tx - d)
            tile = own[plane, row : row + 8]
            if packed and wide:
                tile = jnp.where(low, tile, own[plane, row + 8 : row + 16])
            ref[k] = tile


def read_messages(targets, a_ref, b_ref, tx, ty, reach):
    odd = lax.axis_index("gx") % 2
    wide = targets[0].shape[1] == ty + 16
    for k, (field, d, row, packed) in enumerate(message_tiles(len(targets), tx, ty, reach)):
        for ref, below in ((a_ref, odd), (b_ref, 1 - odd)):
            plane = below * (tx - d) + (1 - below) * (2 * tx + d - 1)
            tile = ref[k]
            targets[field][plane, row : row + 8] = tile
            if packed and wide:
                targets[field][plane, row + 8 : row + 16] = tile


def join_kernel(fields, tx, ty, state_ref, y_a, y_b, own_ref, a_ref, b_ref):
    odd = lax.axis_index("gy") % 2
    own_ref[:, 0:ty] = state_ref[...]
    own_ref[:, pl.ds(pl.multiple_of(ty + 8 * odd, 8), 8)] = y_a[...]
    own_ref[:, pl.ds(pl.multiple_of(ty + 8 - 8 * odd, 8), 8)] = y_b[...]
    write_messages(own_ref, a_ref, b_ref, fields, tx, ty, 2 * W)


def shifted(v, axis, by, edge):
    n = v.shape[axis]
    moved = pltpu.roll(v, by % n, axis)
    if not edge:
        return moved
    ids = lax.broadcasted_iota(jnp.int32, v.shape, axis)
    return jnp.where(ids == (0 if by == 1 else n - 1), 0.0, moved)


def neighbours(plane, x):
    v = plane(x)
    total = plane(x - 1) + plane(x + 1)
    total = total + (shifted(v, 0, 1, False) + shifted(v, 0, -1, False))
    return v, total + (shifted(v, 1, 1, True) + shifted(v, 1, -1, True))


def narrow(v, ty):
    above, below = v[..., ty : ty + 8, :], v[..., ty + 8 :, :]
    low = lax.broadcasted_iota(jnp.int32, above.shape, above.ndim - 2) < 4
    return jnp.concatenate([v[..., 0:ty, :], jnp.where(low, above, below)], axis=-2)


def window_kernel(kind, tx, ty, *refs):
    refs = list(refs)
    take = lambda n: [refs.pop(0) for _ in range(n)]
    own, x_a, x_b = take(3)
    (cell_row,) = take(1)
    if kind != "first":
        gain_ref, count_ref = take(2)
    done = take(3) if kind == "last" else ()
    if kind == "last":
        out_cur, out_bef, series_ref = take(3)
    else:
        state_ref, *rest = take(3)
        (sample_ref,) = take(1)
    if kind == "first":
        gain_ref, count_ref, gain4_ref, count4_ref = take(4)
    one, two = take(2)
    nz = own.shape[2]
    targets = [one, two] + ([gain_ref] if kind == "first" else [])
    for field, target in enumerate(targets):
        target[tx : 2 * tx] = own[field * tx : (field + 1) * tx]
    reach = 2 * W if kind in ("first", "wide") else W
    read_messages(targets, x_a, x_b, tx, ty, reach)
    if kind == "first":
        count_ref[...] = jnp.zeros(count_ref.shape, F32)
        opened = lambda i: jnp.where(gain_ref[i] > 0.0, F32(1.0), F32(0.0))
        for x in range(1, 3 * tx - 1):
            count_ref[x] = neighbours(opened, x)[1]
        gain4_ref[...] = narrow(gain_ref[...], ty)
        count4_ref[...] = narrow(count_ref[...], ty)
    cell = cell_row[...]
    safe = jnp.maximum(cell, 0)
    lane = lax.broadcasted_iota(jnp.int32, (1, 128), 1)
    z_of = safe % nz + (lane >= 64).astype(jnp.int32)
    row_of = jnp.where(cell >= 0, safe // nz, -1)
    zhot = (lax.broadcasted_iota(jnp.int32, (nz, 128), 0) == z_of).astype(BF16)
    rhot = lax.broadcasted_iota(jnp.int32, (tx * ty, 128), 0) == row_of

    picks = []
    for step in range(1, W + 1):
        cur, bef = (one, two) if step % 2 else (two, one)
        for x in range(step, 3 * tx - step):
            v, total = neighbours(lambda i: cur[i], x)
            b = bef[x]
            inner = 0.25 * (total - count_ref[x] * v) + 2.0 * (v - b)
            bef[x] = gain_ref[x] * inner + b
        now = bef[tx : 2 * tx, 0:ty].reshape(tx * ty, nz)
        high = now.astype(BF16)
        low = (now - high.astype(F32)).astype(BF16)
        dot = lambda a: jnp.dot(a, zhot, preferred_element_type=F32)
        picked = jnp.where(rhot, dot(high) + dot(low), 0.0)
        picks.append(jnp.sum(picked, axis=0, keepdims=True))
    cur, bef = (one, two) if W % 2 == 0 else (two, one)
    cur, bef = cur.at[tx : 2 * tx], bef.at[tx : 2 * tx]
    if kind == "last":
        out_cur[...] = cur[:, 0:ty]
        out_bef[...] = bef[:, 0:ty]
        cells = jnp.broadcast_to(cell.astype(F32), (8, 128))
        series = jnp.concatenate([*(d[...] for d in done), *picks, cells])
        for d in range(series_ref.shape[0]):
            series_ref[d] = series
        return
    for k, pick in enumerate(picks):
        sample_ref[pl.ds(k, 1), :] = pick
    if kind == "inner":
        state_ref[0:tx] = cur[:, 0:ty]
        state_ref[tx:] = bef[:, 0:ty]
        rest[0][...], rest[1][...] = edges(state_ref, ty)
    else:
        state_ref[0:tx] = narrow(cur[...], ty)
        state_ref[tx:] = narrow(bef[...], ty)
        write_messages(state_ref, *rest, 2, tx, ty, W)


def sin_cos_turns(p):
    r = p - jnp.floor(p + 0.5)
    q = r * r
    s = F32(-0.00702838626472677)
    for k in (0.0820504017189708, -0.599252197803835, 2.55016331894515, -5.16771276462447, 3.14159265353629):
        s = s * q + F32(k)
    s = s * r
    c = F32(-0.0243963243010939)
    for k in (0.234937313786045, -1.33521200304381, 4.0587091595557, -4.93480213707881, 0.999999999779904):
        c = c * q + F32(k)
    return 2.0 * s * c, 1.0 - 2.0 * s * s


def project_kernel(tx, ty, nz, own, series_ref, angle_ref, out_ref):
    slots = 64
    ndev, _, lanes = series_ref.shape
    at = pl.multiple_of(lax.axis_index("gy") * own, 128)
    sin_e, cos_e = sin_cos_turns(angle_ref[0:1, pl.ds(at, own)] * (1.0 / TURN))
    sin_a, cos_a = sin_cos_turns(angle_ref[1:2, pl.ds(at, own)] * (1.0 / TURN))
    ux, uy, uz = cos_e * cos_a, cos_e * sin_a, sin_e
    rows = [series_ref[d, STEPS : STEPS + 1, :] for d in range(ndev)]
    cells = jnp.concatenate([*rows, jnp.zeros((lanes - ndev, lanes), F32)]).T[0:slots]
    cells = jnp.maximum(cells, 0.0).astype(jnp.int32)
    device = lax.broadcasted_iota(jnp.int32, cells.shape, 1)
    x_of = (lax.axis_index("gx") * tx + cells // (ty * nz)).astype(F32)
    y_of = (device * ty + cells // nz % ty).astype(F32)
    z_of = (cells % nz).astype(F32)
    total = jnp.zeros((STEPS, own), F32)
    for d in range(ndev):
        column = lambda v: v[:, d : d + 1]
        turns = (KAPPA / TURN) * (ux * column(x_of) + uy * column(y_of) + uz * column(z_of))
        s, c = sin_cos_turns(turns)
        waves = jnp.concatenate([uz * s - c, c])
        wave_high = waves.astype(BF16)
        wave_low = (waves - wave_high.astype(F32)).astype(BF16)
        v = series_ref[d, 0:STEPS, :]
        high = v.astype(BF16)
        low = (v - high.astype(F32)).astype(BF16)
        dot = lambda a, b: jnp.dot(a, b, preferred_element_type=F32)
        total = total + dot(high, wave_high) + (dot(low, wave_high) + dot(high, wave_low))
    for k in range(out_ref.shape[0]):
        out_ref[k] = total


def total_kernel(part_ref, out_ref):
    out_ref[...] = jnp.sum(part_ref[...], axis=0)


def spectra_kernel(scale, bin_total, trace_ref, other_ref, spec_ref, out_ref):
    bins = spec_ref.shape[1]
    period = 2 * (bin_total + 1)
    bin_of = lax.axis_index("gx") * bins + lax.broadcasted_iota(jnp.int32, (bins, STEPS), 0) + 1
    step_of = lax.broadcasted_iota(jnp.int32, (bins, STEPS), 1) + START
    turn = (step_of * bin_of).astype(F32)
    turn = turn - period * jnp.floor(turn * (1.0 / period))
    sin_t, cos_t = sin_cos_turns(turn * (1.0 / period))
    traces = (trace_ref[...] + other_ref[...]) * F32(scale)
    dot = lambda a: jnp.dot(a, traces, preferred_element_type=F32, precision=lax.Precision.HIGHEST)
    out_ref[0] = spec_ref[0] + dot(cos_t)
    out_ref[1] = spec_ref[1] - dot(sin_t)


def swap(v, axis):
    count = lax.axis_size(axis)
    even_odd = [(i, i ^ 1) for i in range(count) if i ^ 1 < count]
    odd_even = [(i, ((i + 1) ^ 1) - 1) for i in range(1, count) if ((i + 1) ^ 1) - 1 < count]
    v_a, v_b = v
    got_b = lax.ppermute(v_b, axis, odd_even)
    return lax.ppermute(v_a, axis, even_odd), got_b


def body(pressure, previous, material, slot_cell, angles, spectra_in):
    tx, ty, nz = pressure.shape
    ngx, ngy = lax.axis_size("gx"), lax.axis_size("gy")
    shape = lambda *s: jax.ShapeDtypeStruct(s, F32)
    window = lambda kind: lambda *refs: window_kernel(kind, tx, ty, *refs)
    wide, thin = (3 * tx, ty + 2 * Y, nz), (3 * tx, ty + 2 * W, nz)
    scratch = lambda s: [pltpu.VMEM(s, F32)] * 2

    def exchange_y(fields, state, a, b):
        size = shape(len(message_tiles(fields, tx, ty, 2 * W)), 8, nz)
        return call(
            lambda *refs: join_kernel(fields, tx, ty, *refs), [shape(fields * tx, *wide[1:]), size, size], name="join"
        )(state, *swap((a, b), "gy"))

    def exchange_x(own, a, b):
        return [own, *swap((a, b), "gx"), cells]

    cells = jnp.concatenate([slot_cell, slot_cell])[None, :]
    tile, edge = (tx, ty, nz), (tx, Y, nz)
    hbm = pl.BlockSpec(memory_space=pltpu.HBM)
    state = call(
        prepare_kernel,
        [shape(3 * tx, ty, nz), shape(3 * tx, Y, nz), shape(3 * tx, Y, nz)],
        [pltpu.VMEM(tile, F32), pltpu.VMEM(tile, F32), pltpu.VMEM(tile, jnp.int32), pltpu.SemaphoreType.DMA((3,))],
        name="prepare",
        specs=[hbm] * 3,
    )(*(pltpu.with_memory_space_constraint(v, pltpu.HBM) for v in (pressure, previous, material)))
    own = exchange_y(3, *state)
    part = shape(W, 128)
    message = shape(len(message_tiles(2, tx, ty, W)), 8, nz)
    between = [shape(2 * tx, *thin[1:]), message, message, part]
    *own, first, gain, count, gain4, count4 = call(
        window("first"), between + [shape(*wide), shape(*wide), shape(*thin), shape(*thin)], scratch(wide), name="window_first"
    )(*exchange_x(*own))
    *state, second = call(
        window("inner"), [shape(2 * tx, ty, nz), shape(2 * tx, Y, nz), shape(2 * tx, Y, nz), part], scratch(thin), name="window_inner"
    )(*exchange_x(*own), gain4, count4)
    own = exchange_y(2, *state)
    *own, third = call(window("wide"), between, scratch(wide), name="window_wide")(*exchange_x(*own), gain, count)
    current, before, series = call(
        window("last"), [shape(*tile), shape(*tile), shape(ngy, STEPS + 8, 128)], scratch(thin), name="window_last"
    )(*exchange_x(*own), gain4, count4, first, second, third)

    series = lax.all_to_all(series, "gy", 0, 0, tiled=True)
    own = spectra_in.shape[2]
    depth = ngx // 4
    groups = [[half * 2 * depth + 2 * z + core for z in range(depth)] for half in range(2) for core in range(2)]
    partial = call(lambda *refs: project_kernel(tx, ty, nz, own, *refs), shape(depth, STEPS, own), name="project")(series, angles)
    partial = lax.all_to_all(partial, "gx", 0, 0, tiled=True, axis_index_groups=groups)
    traces = call(total_kernel, shape(STEPS, own), name="total")(partial)
    traces = traces + lax.ppermute(traces, "gx", [(i, i ^ 1) for i in range(ngx)])
    other = lax.ppermute(traces, "gx", [(i, (i + 2 * depth) % ngx) for i in range(ngx)])
    scale = float(slot_cell.shape[0] * ngx * ngy) ** -0.5
    bins = spectra_in.shape[1] * ngx
    spectra = call(lambda *refs: spectra_kernel(scale, bins, *refs), shape(*spectra_in.shape), name="spectra")(
        traces, other, spectra_in
    )
    return current, before, spectra


def solution(mesh):
    return jax.shard_map(
        body,
        mesh=mesh,
        in_specs=(
            P("gx", "gy", None),
            P("gx", "gy", None),
            P("gx", "gy", None),
            P(("gx", "gy")),
            P(),
            P(None, "gx", "gy"),
        ),
        out_specs=(P("gx", "gy", None), P("gx", "gy", None), P(None, "gx", "gy")),
        check_vma=False,
    )
```

```python
import jax
import jax.numpy as jnp
from jax import lax
from jax.experimental import pallas as pl
from jax.experimental.pallas import tpu as pltpu
from jax.sharding import PartitionSpec as P

STEPS = 16
START = 3000
KAPPA = 0.37
W = 4
Y = 8
F32 = jnp.float32
BF16 = jnp.bfloat16
TURN = 6.283185307179586


def call(kernel, outs, scratch=(), name=None, specs=None):
    more = {} if specs is None else {"in_specs": specs}
    return pl.pallas_call(
        kernel,
        out_shape=outs,
        scratch_shapes=list(scratch),
        compiler_params=pltpu.CompilerParams(vmem_limit_bytes=16 * 1024 * 1024),
        name=name,
        **more,
    )


def plane_sets(fields, tx):
    return [(0, tx), (tx + 1, 2 * tx + 1)] if fields == 2 else [(k * tx, (k + 1) * tx) for k in range(fields)]


def write_edges(state, b_ref, a_ref, fields, tx, ty):
    even = lax.axis_index("gy") % 2 == 0
    top, bottom = ty - Y, 0
    for ref, row in ((a_ref, jnp.where(even, top, bottom)), (b_ref, jnp.where(even, bottom, top))):
        for k, (lo, hi) in enumerate(plane_sets(fields, tx)):
            ref[k * tx : (k + 1) * tx] = state[lo:hi, pl.ds(pl.multiple_of(row, 8), Y)]


def prepare_kernel(cur_hbm, bef_hbm, mat_hbm, state_ref, odd_even_ref, even_odd_ref, cur_ref, bef_ref, mat_ref, sems):
    tx, ty, _ = cur_ref.shape
    pairs = ((mat_hbm, mat_ref), (cur_hbm, cur_ref), (bef_hbm, bef_ref))
    copies = [pltpu.make_async_copy(src, dst, sems.at[k]) for k, (src, dst) in enumerate(pairs)]
    for copy in copies:
        copy.start()
    copies[0].wait()
    mat = mat_ref[...]
    state_ref[2 * tx :] = jnp.where(mat == 1, 0.0, jnp.where(mat == 2, F32(1.0) / F32(1.5), F32(1.0)))
    copies[1].wait()
    state_ref[0:tx] = jnp.where(mat == 1, 0.0, cur_ref[...])
    copies[2].wait()
    state_ref[tx : 2 * tx] = jnp.where(mat == 1, 0.0, bef_ref[...])
    write_edges(state_ref, odd_even_ref, even_odd_ref, 3, tx, ty)


def message_tiles(fields, tx, ty, reach):
    tiles = []
    for field in range(fields):
        late = 1 if field == 1 else 0
        for d in range(1, W + 1 - late):
            known = fields == 2 and late and d == 1
            if not known:
                tiles += [(field, d, 8 * k, False) for k in range(ty // 8)]
            rows = reach - d - late
            if rows > 4:
                tiles += [(field, d, ty, False), (field, d, ty + 8, False)]
            elif rows > 0 and not known:
                tiles.append((field, d, ty, True))
    return tiles


def write_messages(own, b_ref, a_ref, fields, tx, ty, reach):
    odd = lax.axis_index("gx") % 2
    wide = own.shape[1] == ty + 16
    low = lax.broadcasted_iota(jnp.int32, (8, own.shape[2]), 0) < 4
    for k, (field, d, row, packed) in enumerate(message_tiles(fields, tx, ty, reach)):
        for ref, below in ((a_ref, odd), (b_ref, 1 - odd)):
            plane = plane_sets(fields, tx)[field][0] + below * (d - 1) + (1 - below) * (tx - d)
            tile = own[plane, row : row + 8]
            if packed and wide:
                tile = jnp.where(low, tile, own[plane, row + 8 : row + 16])
            ref[k] = tile


def read_messages(targets, b_ref, a_ref, tx, ty, reach):
    odd = lax.axis_index("gx") % 2
    wide = targets[0].shape[1] == ty + 16
    for k, (field, d, row, packed) in enumerate(message_tiles(len(targets), tx, ty, reach)):
        for ref, below in ((a_ref, odd), (b_ref, 1 - odd)):
            plane = below * (tx - d) + (1 - below) * (2 * tx + d - 1)
            tile = ref[k]
            targets[field][plane, row : row + 8] = tile
            if packed and wide:
                targets[field][plane, row + 8 : row + 16] = tile


def join_kernel(fields, tx, ty, state_ref, y_b, y_a, own_ref, odd_even_ref, even_odd_ref):
    odd = lax.axis_index("gy") % 2
    own_ref[:, 0:ty] = state_ref[...]
    for ref, row in ((y_a, ty + 8 * odd), (y_b, ty + 8 - 8 * odd)):
        for k, (lo, hi) in enumerate(plane_sets(fields, tx)):
            own_ref[lo:hi, pl.ds(pl.multiple_of(row, 8), 8)] = ref[k * tx : (k + 1) * tx]
    write_messages(own_ref, odd_even_ref, even_odd_ref, fields, tx, ty, 2 * W)


def around(plane, x):
    v = plane(x)
    lane = lax.broadcasted_iota(jnp.int32, (v.shape[0], 128), 1)
    parts = [v[:, k : k + 128] for k in range(0, v.shape[1], 128)]
    ahead = [pltpu.roll(p, 1, 1) for p in parts]
    back = [pltpu.roll(p, 127, 1) for p in parts]
    below = [jnp.where(lane == 0, a, b) for a, b in zip([0.0, *ahead[:-1]], ahead)]
    above = [jnp.where(lane == 127, a, b) for a, b in zip([*back[1:], 0.0], back)]
    z_sum = jnp.concatenate([a + b for a, b in zip(below, above)], axis=1)
    y_sum = pltpu.roll(v, 1, 0) + pltpu.roll(v, v.shape[0] - 1, 0)
    return v, (plane(x - 1) + plane(x + 1)) + (y_sum + z_sum)


def narrow(v, ty):
    above, below = v[..., ty : ty + 8, :], v[..., ty + 8 :, :]
    low = lax.broadcasted_iota(jnp.int32, above.shape, above.ndim - 2) < 4
    return jnp.concatenate([v[..., 0:ty, :], jnp.where(low, above, below)], axis=-2)


def window_kernel(kind, tx, ty, *refs):
    refs = list(refs)
    take = lambda n: [refs.pop(0) for _ in range(n)]
    own, x_b, x_a = take(3)
    (cell_row,) = take(1)
    if kind != "first":
        coefs = take(3)
    done = take(3) if kind == "last" else ()
    if kind == "last":
        out_cur, out_bef, series_ref = take(3)
    else:
        state_ref, *rest = take(3)
        (sample_ref,) = take(1)
    if kind == "first":
        coefs, coefs4 = take(3), take(3)
        gain_ref = coefs[2]
    one, two = take(2)
    nz = own.shape[2]
    targets = [one, two] + ([gain_ref] if kind == "first" else [])
    if kind == "first":
        for field, target in enumerate(targets):
            target[tx : 2 * tx] = own[field * tx : (field + 1) * tx]
    else:
        one[tx : 2 * tx] = own[0:tx]
        two[tx - 1 : 2 * tx + 1] = own[tx:]
    reach = 2 * W if kind in ("first", "wide") else W
    read_messages(targets, x_b, x_a, tx, ty, reach)
    if kind == "first":
        for k in (0, 1):
            coefs[k][...] = jnp.zeros(coefs[k].shape, F32)
        opened = lambda i: jnp.where(gain_ref[i] > 0.0, F32(1.0), F32(0.0))
        for x in range(1, 3 * tx - 1):
            gain = gain_ref[x]
            coefs[0][x] = gain * (2.0 - 0.25 * around(opened, x)[1])
            coefs[1][x] = 0.25 * gain
        for x in range(3 * tx):
            gain_ref[x] = 1.0 - 2.0 * gain_ref[x]
        for k in range(3):
            coefs4[k][...] = narrow(coefs[k][...], ty)
    cell = cell_row[...]
    safe = jnp.maximum(cell, 0)
    lane = lax.broadcasted_iota(jnp.int32, (1, 128), 1)
    z_of = safe % nz + (lane >= 64).astype(jnp.int32)
    row_of = jnp.where(cell >= 0, safe // nz, -1)
    zhot = (lax.broadcasted_iota(jnp.int32, (nz, 128), 0) == z_of).astype(BF16)
    rhot = lax.broadcasted_iota(jnp.int32, (tx * ty, 128), 0) == row_of

    picks = []
    for step in range(1, W + 1):
        cur, bef = (one, two) if step % 2 else (two, one)
        for x in range(step, 3 * tx - step):
            v, total = around(lambda i: cur[i], x)
            bef[x] = coefs[0][x] * v + coefs[1][x] * total + coefs[2][x] * bef[x]
        now = bef[tx : 2 * tx, 0:ty].reshape(tx * ty, nz)
        high = now.astype(BF16)
        low = (now - high.astype(F32)).astype(BF16)
        dot = lambda a: jnp.dot(a, zhot, preferred_element_type=F32)
        picked = jnp.where(rhot, dot(high) + dot(low), 0.0)
        picks.append(jnp.sum(picked, axis=0, keepdims=True))
    cur, bef = (one, two) if W % 2 == 0 else (two, one)
    if kind == "last":
        out_cur[...] = cur[tx : 2 * tx, 0:ty]
        out_bef[...] = bef[tx : 2 * tx, 0:ty]
        cells = jnp.broadcast_to(cell.astype(F32), (8, 128))
        series = jnp.concatenate([*(d[...] for d in done), *picks, cells])
        for d in range(series_ref.shape[0]):
            series_ref[d] = series
        return
    for k, pick in enumerate(picks):
        sample_ref[pl.ds(k, 1), :] = pick
    cut = (lambda v: v[:, 0:ty]) if kind == "inner" else (lambda v: narrow(v, ty))
    state_ref[0:tx] = cut(cur[tx : 2 * tx])
    state_ref[tx:] = cut(bef[tx - 1 : 2 * tx + 1])
    if kind == "inner":
        write_edges(state_ref, *rest, 2, tx, ty)
    else:
        write_messages(state_ref, *rest, 2, tx, ty, W)


def sin_cos_turns(p):
    r = p - jnp.floor(p + 0.5)
    q = r * r
    s = F32(-0.00702838626472677)
    for k in (0.0820504017189708, -0.599252197803835, 2.55016331894515, -5.16771276462447, 3.14159265353629):
        s = s * q + F32(k)
    s = s * r
    c = F32(-0.0243963243010939)
    for k in (0.234937313786045, -1.33521200304381, 4.0587091595557, -4.93480213707881, 0.999999999779904):
        c = c * q + F32(k)
    return 2.0 * s * c, 1.0 - 2.0 * s * s


def project_kernel(tx, ty, nz, own, series_ref, angle_ref, out_ref):
    slots = 64
    ndev, _, lanes = series_ref.shape
    at = pl.multiple_of(lax.axis_index("gy") * own, 128)
    sin_e, cos_e = sin_cos_turns(angle_ref[0:1, pl.ds(at, own)] * (1.0 / TURN))
    sin_a, cos_a = sin_cos_turns(angle_ref[1:2, pl.ds(at, own)] * (1.0 / TURN))
    ux, uy, uz = cos_e * cos_a, cos_e * sin_a, sin_e
    rows = [series_ref[d, STEPS : STEPS + 1, :] for d in range(ndev)]
    cells = jnp.concatenate([*rows, jnp.zeros((lanes - ndev, lanes), F32)]).T[0:slots]
    cells = jnp.maximum(cells, 0.0).astype(jnp.int32)
    device = lax.broadcasted_iota(jnp.int32, cells.shape, 1)
    x_of = (lax.axis_index("gx") * tx + cells // (ty * nz)).astype(F32)
    y_of = (device * ty + cells // nz % ty).astype(F32)
    z_of = (cells % nz).astype(F32)
    total = jnp.zeros((STEPS, own), F32)
    for d in range(ndev):
        column = lambda v: v[:, d : d + 1]
        turns = (KAPPA / TURN) * (ux * column(x_of) + uy * column(y_of) + uz * column(z_of))
        s, c = sin_cos_turns(turns)
        waves = jnp.concatenate([uz * s - c, c])
        wave_high = waves.astype(BF16)
        wave_low = (waves - wave_high.astype(F32)).astype(BF16)
        v = series_ref[d, 0:STEPS, :]
        high = v.astype(BF16)
        low = (v - high.astype(F32)).astype(BF16)
        dot = lambda a, b: jnp.dot(a, b, preferred_element_type=F32)
        total = total + dot(high, wave_high) + (dot(low, wave_high) + dot(high, wave_low))
    for k in range(out_ref.shape[0]):
        out_ref[k] = total


def total_kernel(part_ref, out_ref):
    out_ref[...] = jnp.sum(part_ref[...], axis=0)


def spectra_kernel(scale, bin_total, trace_ref, other_ref, spec_ref, out_ref):
    bins = spec_ref.shape[1]
    period = 2 * (bin_total + 1)
    bin_of = lax.axis_index("gx") * bins + lax.broadcasted_iota(jnp.int32, (bins, STEPS), 0) + 1
    step_of = lax.broadcasted_iota(jnp.int32, (bins, STEPS), 1) + START
    turn = (step_of * bin_of).astype(F32)
    turn = turn - period * jnp.floor(turn * (1.0 / period))
    sin_t, cos_t = sin_cos_turns(turn * (1.0 / period))
    traces = (trace_ref[...] + other_ref[...]) * F32(scale)
    dot = lambda a: jnp.dot(a, traces, preferred_element_type=F32, precision=lax.Precision.HIGHEST)
    out_ref[0] = spec_ref[0] + dot(cos_t)
    out_ref[1] = spec_ref[1] - dot(sin_t)


def swap(odd_even, even_odd, axis):
    count = lax.axis_size(axis)
    pairs = [(i, ((i + 1) ^ 1) - 1) for i in range(1, count) if ((i + 1) ^ 1) - 1 < count]
    got = lax.ppermute(odd_even, axis, pairs)
    return got, lax.ppermute(even_odd, axis, [(i, i ^ 1) for i in range(count) if i ^ 1 < count])


def body(pressure, previous, material, slot_cell, angles, spectra_in):
    tx, ty, nz = pressure.shape
    ngx, ngy = lax.axis_size("gx"), lax.axis_size("gy")
    shape = lambda *s: jax.ShapeDtypeStruct(s, F32)
    window = lambda kind: lambda *refs: window_kernel(kind, tx, ty, *refs)
    wide, thin = (3 * tx, ty + 2 * Y, nz), (3 * tx, ty + 2 * W, nz)
    scratch = lambda s: [pltpu.VMEM(s, F32)] * 2

    def exchange_y(fields, state, *edges):
        size = shape(len(message_tiles(fields, tx, ty, 2 * W)), 8, nz)
        return call(
            lambda *refs: join_kernel(fields, tx, ty, *refs), [shape(*state.shape[:1], *wide[1:]), size, size], name="join"
        )(state, *swap(*edges, "gy"))

    def exchange_x(own, *messages):
        return [own, *swap(*messages, "gx"), cells]

    cells = jnp.concatenate([slot_cell, slot_cell])[None, :]
    tile, edge = (tx, ty, nz), (tx, Y, nz)
    hbm = pl.BlockSpec(memory_space=pltpu.HBM)
    state = call(
        prepare_kernel,
        [shape(3 * tx, ty, nz), shape(3 * tx, Y, nz), shape(3 * tx, Y, nz)],
        [pltpu.VMEM(tile, F32), pltpu.VMEM(tile, F32), pltpu.VMEM(tile, jnp.int32), pltpu.SemaphoreType.DMA((3,))],
        name="prepare",
        specs=[hbm] * 3,
    )(*(pltpu.with_memory_space_constraint(v, pltpu.HBM) for v in (pressure, previous, material)))
    own = exchange_y(3, *state)
    part = shape(W, 128)
    message = shape(len(message_tiles(2, tx, ty, W)), 8, nz)
    between = [shape(2 * tx + 2, *thin[1:]), message, message, part]
    *own, first, p, q, r, p4, q4, r4 = call(
        window("first"), between + [shape(*wide)] * 3 + [shape(*thin)] * 3, scratch(wide), name="window_first"
    )(*exchange_x(*own))
    *state, second = call(
        window("inner"), [shape(2 * tx + 2, ty, nz), shape(2 * tx, Y, nz), shape(2 * tx, Y, nz), part], scratch(thin), name="window_inner"
    )(*exchange_x(*own), p4, q4, r4)
    own = exchange_y(2, *state)
    *own, third = call(window("wide"), between, scratch(wide), name="window_wide")(*exchange_x(*own), p, q, r)
    current, before, series = call(
        window("last"), [shape(*tile), shape(*tile), shape(ngy, STEPS + 8, 128)], scratch(thin), name="window_last"
    )(*exchange_x(*own), p4, q4, r4, first, second, third)

    series = lax.all_to_all(series, "gy", 0, 0, tiled=True)
    own = spectra_in.shape[2]
    depth = ngx // 4
    groups = [[half * 2 * depth + 2 * z + core for z in range(depth)] for half in range(2) for core in range(2)]
    partial = call(lambda *refs: project_kernel(tx, ty, nz, own, *refs), shape(depth, STEPS, own), name="project")(series, angles)
    partial = lax.all_to_all(partial, "gx", 0, 0, tiled=True, axis_index_groups=groups)
    traces = call(total_kernel, shape(STEPS, own), name="total")(partial)
    traces = traces + lax.ppermute(traces, "gx", [(i, i ^ 1) for i in range(ngx)])
    other = lax.ppermute(traces, "gx", [(i, (i + 2 * depth) % ngx) for i in range(ngx)])
    scale = float(slot_cell.shape[0] * ngx * ngy) ** -0.5
    bins = spectra_in.shape[1] * ngx
    spectra = call(lambda *refs: spectra_kernel(scale, bins, *refs), shape(*spectra_in.shape), name="spectra")(
        traces, other, spectra_in
    )
    return current, before, spectra


def solution(mesh):
    return jax.shard_map(
        body,
        mesh=mesh,
        in_specs=(
            P("gx", "gy", None),
            P("gx", "gy", None),
            P("gx", "gy", None),
            P(("gx", "gy")),
            P(),
            P(None, "gx", "gy"),
        ),
        out_specs=(P("gx", "gy", None), P("gx", "gy", None), P(None, "gx", "gy")),
        check_vma=False,
    )
```

```python
import jax
import jax.numpy as jnp
from jax import lax
from jax.experimental import pallas as pl
from jax.experimental.pallas import tpu as pltpu
from jax.sharding import PartitionSpec as P

STEPS = 16
START = 3000
KAPPA = 0.37
W = 4
Y = 8
F32 = jnp.float32
BF16 = jnp.bfloat16
TURN = 6.283185307179586


def call(kernel, outs, scratch=(), name=None, specs=None):
    more = {} if specs is None else {"in_specs": specs}
    return pl.pallas_call(
        kernel,
        out_shape=outs,
        scratch_shapes=list(scratch),
        compiler_params=pltpu.CompilerParams(vmem_limit_bytes=16 * 1024 * 1024),
        name=name,
        **more,
    )


def plane_sets(fields, tx):
    return [(0, tx), (tx + 1, 2 * tx + 1)] if fields == 2 else [(k * tx, (k + 1) * tx) for k in range(fields)]


def write_edges(state, b_ref, a_ref, fields, tx, ty):
    even = lax.axis_index("gy") % 2 == 0
    top, bottom = ty - Y, 0
    for ref, row in ((a_ref, jnp.where(even, top, bottom)), (b_ref, jnp.where(even, bottom, top))):
        for k, (lo, hi) in enumerate(plane_sets(fields, tx)):
            ref[k * tx : (k + 1) * tx] = state[lo:hi, pl.ds(pl.multiple_of(row, 8), Y)]


def prepare_kernel(cur_hbm, bef_hbm, mat_hbm, state_ref, odd_even_ref, even_odd_ref, cur_ref, bef_ref, mat_ref, sems):
    tx, ty, _ = cur_ref.shape
    pairs = ((mat_hbm, mat_ref), (cur_hbm, cur_ref), (bef_hbm, bef_ref))
    copies = [pltpu.make_async_copy(src, dst, sems.at[k]) for k, (src, dst) in enumerate(pairs)]
    for copy in copies:
        copy.start()
    copies[0].wait()
    mat = mat_ref[...]
    state_ref[2 * tx :] = jnp.where(mat == 1, 0.0, jnp.where(mat == 2, F32(1.0) / F32(1.5), F32(1.0)))
    copies[1].wait()
    state_ref[0:tx] = jnp.where(mat == 1, 0.0, cur_ref[...])
    copies[2].wait()
    state_ref[tx : 2 * tx] = jnp.where(mat == 1, 0.0, bef_ref[...])
    write_edges(state_ref, odd_even_ref, even_odd_ref, 3, tx, ty)


def message_tiles(fields, tx, ty, reach):
    tiles = []
    for field in range(fields):
        late = 1 if field == 1 else 0
        for d in range(1, W + 1 - late):
            known = fields == 2 and late and d == 1
            if not known:
                tiles += [(field, d, 8 * k, False) for k in range(ty // 8)]
            rows = reach - d - late
            if rows > 4:
                tiles += [(field, d, ty, False), (field, d, ty + 8, False)]
            elif rows > 0 and not known:
                tiles.append((field, d, ty, True))
    return tiles


def write_messages(own, b_ref, a_ref, fields, tx, ty, reach):
    odd = lax.axis_index("gx") % 2
    wide = own.shape[1] == ty + 16
    low = lax.broadcasted_iota(jnp.int32, (8, own.shape[2]), 0) < 4
    for k, (field, d, row, packed) in enumerate(message_tiles(fields, tx, ty, reach)):
        for ref, below in ((a_ref, odd), (b_ref, 1 - odd)):
            plane = plane_sets(fields, tx)[field][0] + below * (d - 1) + (1 - below) * (tx - d)
            tile = own[plane, row : row + 8]
            if packed and wide:
                tile = jnp.where(low, tile, own[plane, row + 8 : row + 16])
            ref[k] = tile


def read_messages(targets, b_ref, a_ref, tx, ty, reach):
    odd = lax.axis_index("gx") % 2
    wide = targets[0].shape[1] == ty + 16
    for k, (field, d, row, packed) in enumerate(message_tiles(len(targets), tx, ty, reach)):
        for ref, below in ((a_ref, odd), (b_ref, 1 - odd)):
            plane = below * (tx - d) + (1 - below) * (2 * tx + d - 1)
            tile = ref[k]
            targets[field][plane, row : row + 8] = tile
            if packed and wide:
                targets[field][plane, row + 8 : row + 16] = tile


def join_kernel(fields, tx, ty, state_ref, y_b, y_a, own_ref, odd_even_ref, even_odd_ref):
    odd = lax.axis_index("gy") % 2
    own_ref[:, 0:ty] = state_ref[...]
    for ref, row in ((y_a, ty + 8 * odd), (y_b, ty + 8 - 8 * odd)):
        for k, (lo, hi) in enumerate(plane_sets(fields, tx)):
            own_ref[lo:hi, pl.ds(pl.multiple_of(row, 8), 8)] = ref[k * tx : (k + 1) * tx]
    write_messages(own_ref, odd_even_ref, even_odd_ref, fields, tx, ty, 2 * W)


def around(plane, x):
    v = plane(x)
    lane = lax.broadcasted_iota(jnp.int32, (v.shape[0], 128), 1)
    parts = [v[:, k : k + 128] for k in range(0, v.shape[1], 128)]
    ahead = [pltpu.roll(p, 1, 1) for p in parts]
    back = [pltpu.roll(p, 127, 1) for p in parts]
    below = [jnp.where(lane == 0, a, b) for a, b in zip([0.0, *ahead[:-1]], ahead)]
    above = [jnp.where(lane == 127, a, b) for a, b in zip([*back[1:], 0.0], back)]
    z_sum = jnp.concatenate([a + b for a, b in zip(below, above)], axis=1)
    y_sum = pltpu.roll(v, 1, 0) + pltpu.roll(v, v.shape[0] - 1, 0)
    return v, (plane(x - 1) + plane(x + 1)) + (y_sum + z_sum)


def advance_step(cur, bef, coefs, lo, hi):
    rows = cur.shape[1] // 8
    row = lax.broadcasted_iota(jnp.int32, (8, 128), 0)
    lane = lax.broadcasted_iota(jnp.int32, (8, 128), 1)
    n = cur.shape[2] // 128
    for k in range(rows):
        before, after = (k - 1) % rows, (k + 1) % rows
        at = slice(8 * k, 8 * k + 8)
        load = lambda x, i, j: cur[x, 8 * i : 8 * i + 8, 128 * j : 128 * j + 128]
        line = lambda x: [load(x, k, j) for j in range(n)]
        down, here = line(lo - 1), line(lo)
        for x in range(lo, hi):
            up = line(x + 1)
            ahead = [pltpu.roll(p, 1, 1) for p in here]
            back = [pltpu.roll(p, 127, 1) for p in here]
            for j in range(n):
                cols = slice(128 * j, 128 * j + 128)
                z = jnp.where(lane == 0, ahead[j - 1] if j else 0.0, ahead[j])
                z = z + jnp.where(lane == 127, back[j + 1] if j + 1 < n else 0.0, back[j])
                y = pltpu.roll(jnp.where(row == 7, load(x, before, j), here[j]), 1, 0)
                y = y + pltpu.roll(jnp.where(row == 0, load(x, after, j), here[j]), 7, 0)
                total = (down[j] + up[j]) + (y + z)
                new = coefs[0][x, at, cols] * here[j] + coefs[1][x, at, cols] * total
                bef[x, at, cols] = new + coefs[2][x, at, cols] * bef[x, at, cols]
            down, here = here, up


def narrow(v, ty):
    above, below = v[..., ty : ty + 8, :], v[..., ty + 8 :, :]
    low = lax.broadcasted_iota(jnp.int32, above.shape, above.ndim - 2) < 4
    return jnp.concatenate([v[..., 0:ty, :], jnp.where(low, above, below)], axis=-2)


def window_kernel(kind, tx, ty, *refs):
    refs = list(refs)
    take = lambda n: [refs.pop(0) for _ in range(n)]
    own, x_b, x_a = take(3)
    (cell_row,) = take(1)
    if kind != "first":
        coefs = take(3)
    done = take(3) if kind == "last" else ()
    if kind == "last":
        out_cur, out_bef, series_ref = take(3)
    else:
        state_ref, *rest = take(3)
        (sample_ref,) = take(1)
    if kind == "first":
        coefs, coefs4 = take(3), take(3)
        gain_ref = coefs[2]
    one, two = take(2)
    nz = own.shape[2]
    targets = [one, two] + ([gain_ref] if kind == "first" else [])
    if kind == "first":
        for field, target in enumerate(targets):
            target[tx : 2 * tx] = own[field * tx : (field + 1) * tx]
    else:
        one[tx : 2 * tx] = own[0:tx]
        two[tx - 1 : 2 * tx + 1] = own[tx:]
    reach = 2 * W if kind in ("first", "wide") else W
    read_messages(targets, x_b, x_a, tx, ty, reach)
    if kind == "first":
        for k in (0, 1):
            coefs[k][...] = jnp.zeros(coefs[k].shape, F32)
        opened = lambda i: jnp.where(gain_ref[i] > 0.0, F32(1.0), F32(0.0))
        for x in range(1, 3 * tx - 1):
            gain = gain_ref[x]
            coefs[0][x] = gain * (2.0 - 0.25 * around(opened, x)[1])
            coefs[1][x] = 0.25 * gain
        for x in range(3 * tx):
            gain_ref[x] = 1.0 - 2.0 * gain_ref[x]
        for k in range(3):
            coefs4[k][...] = narrow(coefs[k][...], ty)
    cell = cell_row[...]
    safe = jnp.maximum(cell, 0)
    lane = lax.broadcasted_iota(jnp.int32, (1, 128), 1)
    z_of = safe % nz + (lane >= 64).astype(jnp.int32)
    row_of = jnp.where(cell >= 0, safe // nz, -1)
    zhot = (lax.broadcasted_iota(jnp.int32, (nz, 128), 0) == z_of).astype(BF16)
    rhot = lax.broadcasted_iota(jnp.int32, (tx * ty, 128), 0) == row_of

    picks = []
    for step in range(1, W + 1):
        cur, bef = (one, two) if step % 2 else (two, one)
        advance_step(cur, bef, coefs, step, 3 * tx - step)
        now = bef[tx : 2 * tx, 0:ty].reshape(tx * ty, nz)
        high = now.astype(BF16)
        low = (now - high.astype(F32)).astype(BF16)
        dot = lambda a: jnp.dot(a, zhot, preferred_element_type=F32)
        picked = jnp.where(rhot, dot(high) + dot(low), 0.0)
        picks.append(jnp.sum(picked, axis=0, keepdims=True))
    cur, bef = (one, two) if W % 2 == 0 else (two, one)
    if kind == "last":
        out_cur[...] = cur[tx : 2 * tx, 0:ty]
        out_bef[...] = bef[tx : 2 * tx, 0:ty]
        series_ref[...] = jnp.concatenate([*(d[...] for d in done), *picks])
        return
    for k, pick in enumerate(picks):
        sample_ref[pl.ds(k, 1), :] = pick
    cut = (lambda v: v[:, 0:ty]) if kind == "inner" else (lambda v: narrow(v, ty))
    state_ref[0:tx] = cut(cur[tx : 2 * tx])
    state_ref[tx:] = cut(bef[tx - 1 : 2 * tx + 1])
    if kind == "inner":
        write_edges(state_ref, *rest, 2, tx, ty)
    else:
        write_messages(state_ref, *rest, 2, tx, ty, W)


def sin_cos_turns(p):
    r = p - jnp.floor(p + 0.5)
    q = r * r
    s = F32(-0.00702838626472677)
    for k in (0.0820504017189708, -0.599252197803835, 2.55016331894515, -5.16771276462447, 3.14159265353629):
        s = s * q + F32(k)
    s = s * r
    c = F32(-0.0243963243010939)
    for k in (0.234937313786045, -1.33521200304381, 4.0587091595557, -4.93480213707881, 0.999999999779904):
        c = c * q + F32(k)
    return 2.0 * s * c, 1.0 - 2.0 * s * s


def waves_kernel(tx, ty, nz, cell_ref, angle_ref, high_ref, low_ref):
    slots = cell_ref.shape[1] // 2
    cells = jnp.broadcast_to(cell_ref[...], (8, 2 * slots)).astype(F32)
    cells = jnp.concatenate([cells] * (2 * slots // 8)).T[0:slots, 0:1]
    cells = jnp.maximum(cells, 0.0).astype(jnp.int32)
    x_of = (lax.axis_index("gx") * tx + cells // (ty * nz)).astype(F32)
    y_of = (lax.axis_index("gy") * ty + cells // nz % ty).astype(F32)
    z_of = (cells % nz).astype(F32)
    width = 512
    for k in range(0, angle_ref.shape[1], width):
        cols = slice(k, k + width)
        sin_e, cos_e = sin_cos_turns(angle_ref[0:1, cols] * (1.0 / TURN))
        sin_a, cos_a = sin_cos_turns(angle_ref[1:2, cols] * (1.0 / TURN))
        ux, uy, uz = cos_e * cos_a, cos_e * sin_a, sin_e
        s, c = sin_cos_turns((KAPPA / TURN) * (ux * x_of + uy * y_of + uz * z_of))
        for half, v in enumerate((uz * s - c, c)):
            rows = slice(half * slots, (half + 1) * slots)
            high = v.astype(BF16)
            high_ref[rows, cols] = high
            low_ref[rows, cols] = (v - high.astype(F32)).astype(BF16)


def project_kernel(series_ref, high_ref, low_ref, out_ref):
    v = series_ref[...]
    high = v.astype(BF16)
    low = (v - high.astype(F32)).astype(BF16)
    dot = lambda a, b: jnp.dot(a, b, preferred_element_type=F32)
    both = dot(jnp.concatenate([high, low]), high_ref[...])
    total = (both[STEPS:] + dot(high, low_ref[...])) + both[0:STEPS]
    ngy = out_ref.shape[0] // 2
    for core in range(2):
        for j in range(ngy):
            at = (2 * j + core) * 128
            out_ref[core * ngy + j] = total[:, at : at + 128]


def total_kernel(part_ref, out_ref):
    total = jnp.sum(part_ref[...], axis=0)
    for k in range(out_ref.shape[0]):
        out_ref[k] = total


def spectra_kernel(scale, bin_total, trace_ref, other_ref, spec_ref, out_ref):
    bins = spec_ref.shape[1]
    period = 2 * (bin_total + 1)
    bin_of = lax.axis_index("gx") * bins + lax.broadcasted_iota(jnp.int32, (bins, STEPS), 0) + 1
    step_of = lax.broadcasted_iota(jnp.int32, (bins, STEPS), 1) + START
    turn = (step_of * bin_of).astype(F32)
    turn = turn - period * jnp.floor(turn * (1.0 / period))
    sin_t, cos_t = sin_cos_turns(turn * (1.0 / period))
    dot = lambda a, b: jnp.dot(a, b, preferred_element_type=F32, precision=lax.Precision.HIGHEST)
    core = lax.axis_index("gx") % 2
    for traces, half in ((trace_ref[0], core), (other_ref[0], 1 - core)):
        at = pl.ds(pl.multiple_of(half * 128, 128), 128)
        traces = traces * F32(scale)
        out_ref[0, :, at] = spec_ref[0, :, at] + dot(cos_t, traces)
        out_ref[1, :, at] = spec_ref[1, :, at] - dot(sin_t, traces)


def swap(odd_even, even_odd, axis):
    count = lax.axis_size(axis)
    pairs = [(i, ((i + 1) ^ 1) - 1) for i in range(1, count) if ((i + 1) ^ 1) - 1 < count]
    got = lax.ppermute(odd_even, axis, pairs)
    return got, lax.ppermute(even_odd, axis, [(i, i ^ 1) for i in range(count) if i ^ 1 < count])


def body(pressure, previous, material, slot_cell, angles, spectra_in):
    tx, ty, nz = pressure.shape
    ngx, ngy = lax.axis_size("gx"), lax.axis_size("gy")
    shape = lambda *s: jax.ShapeDtypeStruct(s, F32)
    window = lambda kind: lambda *refs: window_kernel(kind, tx, ty, *refs)
    wide, thin = (3 * tx, ty + 2 * Y, nz), (3 * tx, ty + 2 * W, nz)
    scratch = lambda s: [pltpu.VMEM(s, F32)] * 2

    def exchange_y(fields, state, *edges):
        size = shape(len(message_tiles(fields, tx, ty, 2 * W)), 8, nz)
        return call(
            lambda *refs: join_kernel(fields, tx, ty, *refs), [shape(*state.shape[:1], *wide[1:]), size, size], name="join"
        )(state, *swap(*edges, "gy"))

    def exchange_x(own, *messages):
        return [own, *swap(*messages, "gx"), cells]

    cells = jnp.concatenate([slot_cell, slot_cell])[None, :]
    tile, edge = (tx, ty, nz), (tx, Y, nz)
    hbm = pl.BlockSpec(memory_space=pltpu.HBM)
    state = call(
        prepare_kernel,
        [shape(3 * tx, ty, nz), shape(3 * tx, Y, nz), shape(3 * tx, Y, nz)],
        [pltpu.VMEM(tile, F32), pltpu.VMEM(tile, F32), pltpu.VMEM(tile, jnp.int32), pltpu.SemaphoreType.DMA((3,))],
        name="prepare",
        specs=[hbm] * 3,
    )(*(pltpu.with_memory_space_constraint(v, pltpu.HBM) for v in (pressure, previous, material)))
    own = exchange_y(3, *state)
    part = shape(W, 128)
    message = shape(len(message_tiles(2, tx, ty, W)), 8, nz)
    between = [shape(2 * tx + 2, *thin[1:]), message, message, part]
    *own, first, p, q, r, p4, q4, r4 = call(
        window("first"), between + [shape(*wide)] * 3 + [shape(*thin)] * 3, scratch(wide), name="window_first"
    )(*exchange_x(*own))
    *state, second = call(
        window("inner"), [shape(2 * tx + 2, ty, nz), shape(2 * tx, Y, nz), shape(2 * tx, Y, nz), part], scratch(thin), name="window_inner"
    )(*exchange_x(*own), p4, q4, r4)
    own = exchange_y(2, *state)
    *own, third = call(window("wide"), between, scratch(wide), name="window_wide")(*exchange_x(*own), p, q, r)
    current, before, series = call(
        window("last"), [shape(*tile), shape(*tile), shape(STEPS, 128)], scratch(thin), name="window_last"
    )(*exchange_x(*own), p4, q4, r4, first, second, third)

    observers = angles.shape[1]
    half = jax.ShapeDtypeStruct((128, observers), BF16)
    high, low = call(lambda *refs: waves_kernel(tx, ty, nz, *refs), [half, half], name="waves")(cells, angles)
    share = call(project_kernel, shape(2 * ngy, STEPS, 128), name="project")(series, high, low)
    rows = [list(range(k, k + 2 * ngy)) for k in range(0, ngx * ngy, 2 * ngy)]
    share = lax.all_to_all(share, ("gx", "gy"), 0, 0, tiled=True, axis_index_groups=rows)
    share = call(total_kernel, shape(ngx // 2, STEPS, 128), name="row_total")(share)
    chips = [list(range(core, ngx, 2)) for core in range(2)]
    share = lax.all_to_all(share, "gx", 0, 0, tiled=True, axis_index_groups=chips)
    traces = call(total_kernel, shape(1, STEPS, 128), name="total")(share)
    other = lax.ppermute(traces, "gx", [(i, i ^ 1) for i in range(ngx)])
    scale = float(slot_cell.shape[0] * ngx * ngy) ** -0.5
    bins = spectra_in.shape[1] * ngx
    spectra = call(lambda *refs: spectra_kernel(scale, bins, *refs), shape(*spectra_in.shape), name="spectra")(
        traces, other, spectra_in
    )
    return current, before, spectra


def solution(mesh):
    return jax.shard_map(
        body,
        mesh=mesh,
        in_specs=(
            P("gx", "gy", None),
            P("gx", "gy", None),
            P("gx", "gy", None),
            P(("gx", "gy")),
            P(),
            P(None, "gx", "gy"),
        ),
        out_specs=(P("gx", "gy", None), P("gx", "gy", None), P(None, "gx", "gy")),
        check_vma=False,
    )
```

```python
import jax
import jax.numpy as jnp
from jax import lax
from jax.experimental import pallas as pl
from jax.experimental.pallas import tpu as pltpu
from jax.sharding import PartitionSpec as P

STEPS = 16
START = 3000
KAPPA = 0.37
W = 4
Y = 8
F32 = jnp.float32
BF16 = jnp.bfloat16
TURN = 6.283185307179586


def call(kernel, outs, scratch=(), name=None, specs=None):
    more = {} if specs is None else {"in_specs": specs}
    return pl.pallas_call(
        kernel,
        out_shape=outs,
        scratch_shapes=list(scratch),
        compiler_params=pltpu.CompilerParams(vmem_limit_bytes=16 * 1024 * 1024),
        name=name,
        **more,
    )


def plane_sets(fields, tx):
    return [(0, tx), (tx + 1, 2 * tx + 1)] if fields == 2 else [(k * tx, (k + 1) * tx) for k in range(fields)]


def write_edges(state, b_ref, a_ref, fields, tx, ty):
    even = lax.axis_index("gy") % 2 == 0
    top, bottom = ty - Y, 0
    for ref, row in ((a_ref, jnp.where(even, top, bottom)), (b_ref, jnp.where(even, bottom, top))):
        for k, (lo, hi) in enumerate(plane_sets(fields, tx)):
            ref[k * tx : (k + 1) * tx] = state[lo:hi, pl.ds(pl.multiple_of(row, 8), Y)]


def prepare_kernel(cur_hbm, bef_hbm, mat_hbm, state_ref, y_b, y_a, x_b, x_a, cur_ref, bef_ref, mat_ref, sems):
    tx, ty, _ = cur_ref.shape
    pairs = ((mat_hbm, mat_ref), (cur_hbm, cur_ref), (bef_hbm, bef_ref))
    copies = [pltpu.make_async_copy(src, dst, sems.at[k]) for k, (src, dst) in enumerate(pairs)]
    for copy in copies:
        copy.start()
    copies[0].wait()
    mat = mat_ref[...]
    state_ref[2 * tx :] = jnp.where(mat == 1, 0.0, jnp.where(mat == 2, F32(1.0) / F32(1.5), F32(1.0)))
    copies[1].wait()
    state_ref[0:tx] = jnp.where(mat == 1, 0.0, cur_ref[...])
    copies[2].wait()
    state_ref[tx : 2 * tx] = jnp.where(mat == 1, 0.0, bef_ref[...])
    write_edges(state_ref, y_b, y_a, 3, tx, ty)
    write_messages(state_ref, x_b, x_a, split_tiles(3, tx, ty, 2 * W)[0], 3, tx, ty)


def message_tiles(fields, tx, ty, reach):
    tiles = []
    for field in range(fields):
        late = 1 if field == 1 else 0
        for d in range(1, W + 1 - late):
            known = fields == 2 and late and d == 1
            if not known:
                tiles += [(field, d, 8 * k, False) for k in range(ty // 8)]
            rows = reach - d - late
            if rows > 4:
                tiles += [(field, d, ty, False), (field, d, ty + 8, False)]
            elif rows > 0 and not known:
                tiles.append((field, d, ty, True))
    return tiles


def split_tiles(fields, tx, ty, reach):
    tiles = message_tiles(fields, tx, ty, reach)
    return [t for t in tiles if t[2] < ty], [t for t in tiles if t[2] >= ty]


def joined_tiles(fields, tx, ty):
    return split_tiles(fields, tx, ty, 2 * W)[1] if fields == 3 else message_tiles(fields, tx, ty, 2 * W)


def write_messages(own, b_ref, a_ref, tiles, fields, tx, ty):
    odd = lax.axis_index("gx") % 2
    wide = own.shape[1] == ty + 16
    low = lax.broadcasted_iota(jnp.int32, (8, own.shape[2]), 0) < 4
    for k, (field, d, row, packed) in enumerate(tiles):
        for ref, below in ((a_ref, odd), (b_ref, 1 - odd)):
            plane = plane_sets(fields, tx)[field][0] + below * (d - 1) + (1 - below) * (tx - d)
            tile = own[plane, row : row + 8]
            if packed and wide:
                tile = jnp.where(low, tile, own[plane, row + 8 : row + 16])
            ref[k] = tile


def read_messages(targets, b_ref, a_ref, tiles, tx, ty):
    odd = lax.axis_index("gx") % 2
    wide = targets[0].shape[1] == ty + 16
    for k, (field, d, row, packed) in enumerate(tiles):
        for ref, below in ((a_ref, odd), (b_ref, 1 - odd)):
            plane = below * (tx - d) + (1 - below) * (2 * tx + d - 1)
            tile = ref[k]
            targets[field][plane, row : row + 8] = tile
            if packed and wide:
                targets[field][plane, row + 8 : row + 16] = tile


def join_kernel(fields, tx, ty, state_ref, y_b, y_a, own_ref, odd_even_ref, even_odd_ref):
    odd = lax.axis_index("gy") % 2
    own_ref[:, 0:ty] = state_ref[...]
    for ref, row in ((y_a, ty + 8 * odd), (y_b, ty + 8 - 8 * odd)):
        for k, (lo, hi) in enumerate(plane_sets(fields, tx)):
            own_ref[lo:hi, pl.ds(pl.multiple_of(row, 8), 8)] = ref[k * tx : (k + 1) * tx]
    write_messages(own_ref, odd_even_ref, even_odd_ref, joined_tiles(fields, tx, ty), fields, tx, ty)


def around(plane, x):
    v = plane(x)
    lane = lax.broadcasted_iota(jnp.int32, (v.shape[0], 128), 1)
    parts = [v[:, k : k + 128] for k in range(0, v.shape[1], 128)]
    ahead = [pltpu.roll(p, 1, 1) for p in parts]
    back = [pltpu.roll(p, 127, 1) for p in parts]
    below = [jnp.where(lane == 0, a, b) for a, b in zip([0.0, *ahead[:-1]], ahead)]
    above = [jnp.where(lane == 127, a, b) for a, b in zip([*back[1:], 0.0], back)]
    z_sum = jnp.concatenate([a + b for a, b in zip(below, above)], axis=1)
    y_sum = pltpu.roll(v, 1, 0) + pltpu.roll(v, v.shape[0] - 1, 0)
    return v, (plane(x - 1) + plane(x + 1)) + (y_sum + z_sum)


def advance_step(cur, bef, coefs, lo, hi):
    rows = cur.shape[1] // 8
    row = lax.broadcasted_iota(jnp.int32, (8, 128), 0)
    lane = lax.broadcasted_iota(jnp.int32, (8, 128), 1)
    n = cur.shape[2] // 128
    for k in range(rows):
        before, after = (k - 1) % rows, (k + 1) % rows
        at = slice(8 * k, 8 * k + 8)
        load = lambda x, i, j: cur[x, 8 * i : 8 * i + 8, 128 * j : 128 * j + 128]
        line = lambda x: [load(x, k, j) for j in range(n)]
        down, here = line(lo - 1), line(lo)
        for x in range(lo, hi):
            up = line(x + 1)
            ahead = [pltpu.roll(p, 1, 1) for p in here]
            back = [pltpu.roll(p, 127, 1) for p in here]
            for j in range(n):
                cols = slice(128 * j, 128 * j + 128)
                z = jnp.where(lane == 0, ahead[j - 1] if j else 0.0, ahead[j])
                z = z + jnp.where(lane == 127, back[j + 1] if j + 1 < n else 0.0, back[j])
                y = pltpu.roll(jnp.where(row == 7, load(x, before, j), here[j]), 1, 0)
                y = y + pltpu.roll(jnp.where(row == 0, load(x, after, j), here[j]), 7, 0)
                total = (down[j] + up[j]) + (y + z)
                new = coefs[0][x, at, cols] * here[j] + coefs[1][x, at, cols] * total
                bef[x, at, cols] = new + coefs[2][x, at, cols] * bef[x, at, cols]
            down, here = here, up


def narrow(v, ty):
    above, below = v[..., ty : ty + 8, :], v[..., ty + 8 :, :]
    low = lax.broadcasted_iota(jnp.int32, above.shape, above.ndim - 2) < 4
    return jnp.concatenate([v[..., 0:ty, :], jnp.where(low, above, below)], axis=-2)


def window_kernel(kind, tx, ty, *refs):
    refs = list(refs)
    take = lambda n: [refs.pop(0) for _ in range(n)]
    own, x_b, x_a = take(3)
    from_y = take(2) if kind == "first" else ()
    (cell_row,) = take(1)
    if kind != "first":
        coefs = take(3)
    done = take(3) if kind == "last" else ()
    if kind == "last":
        out_cur, out_bef, series_ref = take(3)
    else:
        state_ref, *rest = take(3)
        (sample_ref,) = take(1)
    if kind == "first":
        coefs, coefs4 = take(3), take(3)
        gain_ref = coefs[2]
    one, two = take(2)
    nz = own.shape[2]
    targets = [one, two] + ([gain_ref] if kind == "first" else [])
    if kind == "first":
        for field, target in enumerate(targets):
            target[tx : 2 * tx] = own[field * tx : (field + 1) * tx]
    else:
        one[tx : 2 * tx] = own[0:tx]
        two[tx - 1 : 2 * tx + 1] = own[tx:]
    if from_y:
        for pair, tiles in zip(((x_b, x_a), from_y), split_tiles(len(targets), tx, ty, 2 * W)):
            read_messages(targets, *pair, tiles, tx, ty)
    else:
        read_messages(targets, x_b, x_a, message_tiles(2, tx, ty, 2 * W if kind == "wide" else W), tx, ty)
    if kind == "first":
        for k in (0, 1):
            coefs[k][...] = jnp.zeros(coefs[k].shape, F32)
        opened = lambda i: jnp.where(gain_ref[i] > 0.0, F32(1.0), F32(0.0))
        for x in range(1, 3 * tx - 1):
            gain = gain_ref[x]
            coefs[0][x] = gain * (2.0 - 0.25 * around(opened, x)[1])
            coefs[1][x] = 0.25 * gain
        for x in range(3 * tx):
            gain_ref[x] = 1.0 - 2.0 * gain_ref[x]
        for k in range(3):
            coefs4[k][...] = narrow(coefs[k][...], ty)
    cell = cell_row[...]
    safe = jnp.maximum(cell, 0)
    lane = lax.broadcasted_iota(jnp.int32, (1, 128), 1)
    z_of = safe % nz + (lane >= 64).astype(jnp.int32)
    row_of = jnp.where(cell >= 0, safe // nz, -1)
    zhot = (lax.broadcasted_iota(jnp.int32, (nz, 128), 0) == z_of).astype(BF16)
    rhot = lax.broadcasted_iota(jnp.int32, (tx * ty, 128), 0) == row_of

    picks = []
    for step in range(1, W + 1):
        cur, bef = (one, two) if step % 2 else (two, one)
        advance_step(cur, bef, coefs, step, 3 * tx - step)
        now = bef[tx : 2 * tx, 0:ty].reshape(tx * ty, nz)
        high = now.astype(BF16)
        low = (now - high.astype(F32)).astype(BF16)
        dot = lambda a: jnp.dot(a, zhot, preferred_element_type=F32)
        picked = jnp.where(rhot, dot(high) + dot(low), 0.0)
        picks.append(jnp.sum(picked, axis=0, keepdims=True))
    cur, bef = (one, two) if W % 2 == 0 else (two, one)
    if kind == "last":
        out_cur[...] = cur[tx : 2 * tx, 0:ty]
        out_bef[...] = bef[tx : 2 * tx, 0:ty]
        series_ref[...] = jnp.concatenate([*(d[...] for d in done), *picks])
        return
    for k, pick in enumerate(picks):
        sample_ref[pl.ds(k, 1), :] = pick
    cut = (lambda v: v[:, 0:ty]) if kind == "inner" else (lambda v: narrow(v, ty))
    state_ref[0:tx] = cut(cur[tx : 2 * tx])
    state_ref[tx:] = cut(bef[tx - 1 : 2 * tx + 1])
    if kind == "inner":
        write_edges(state_ref, *rest, 2, tx, ty)
    else:
        write_messages(state_ref, *rest, message_tiles(2, tx, ty, W), 2, tx, ty)


def sin_cos_turns(p):
    r = p - jnp.floor(p + 0.5)
    q = r * r
    s = F32(-0.00702838626472677)
    for k in (0.0820504017189708, -0.599252197803835, 2.55016331894515, -5.16771276462447, 3.14159265353629):
        s = s * q + F32(k)
    s = s * r
    c = F32(-0.0243963243010939)
    for k in (0.234937313786045, -1.33521200304381, 4.0587091595557, -4.93480213707881, 0.999999999779904):
        c = c * q + F32(k)
    return 2.0 * s * c, 1.0 - 2.0 * s * s


def waves_kernel(tx, ty, nz, cell_ref, angle_ref, high_ref, low_ref):
    slots = cell_ref.shape[1] // 2
    cells = jnp.broadcast_to(cell_ref[...], (8, 2 * slots)).astype(F32)
    cells = jnp.concatenate([cells] * (2 * slots // 8)).T[0:slots, 0:1]
    cells = jnp.maximum(cells, 0.0).astype(jnp.int32)
    x_of = (lax.axis_index("gx") * tx + cells // (ty * nz)).astype(F32)
    y_of = (lax.axis_index("gy") * ty + cells // nz % ty).astype(F32)
    z_of = (cells % nz).astype(F32)
    width = 512
    for k in range(0, angle_ref.shape[1], width):
        cols = slice(k, k + width)
        sin_e, cos_e = sin_cos_turns(angle_ref[0:1, cols] * (1.0 / TURN))
        sin_a, cos_a = sin_cos_turns(angle_ref[1:2, cols] * (1.0 / TURN))
        ux, uy, uz = cos_e * cos_a, cos_e * sin_a, sin_e
        s, c = sin_cos_turns((KAPPA / TURN) * (ux * x_of + uy * y_of + uz * z_of))
        for half, v in enumerate((uz * s - c, c)):
            rows = slice(half * slots, (half + 1) * slots)
            high = v.astype(BF16)
            high_ref[rows, cols] = high
            low_ref[rows, cols] = (v - high.astype(F32)).astype(BF16)


def project_kernel(series_ref, high_ref, low_ref, out_ref):
    v = series_ref[...]
    high = v.astype(BF16)
    low = (v - high.astype(F32)).astype(BF16)
    dot = lambda a, b: jnp.dot(a, b, preferred_element_type=F32)
    both = dot(jnp.concatenate([high, low]), high_ref[...])
    total = (both[STEPS:] + dot(high, low_ref[...])) + both[0:STEPS]
    ngy = out_ref.shape[0] // 2
    for core in range(2):
        for j in range(ngy):
            at = (2 * j + core) * 128
            out_ref[core * ngy + j] = total[:, at : at + 128]


def total_kernel(part_ref, out_ref):
    total = jnp.sum(part_ref[...], axis=0)
    for k in range(out_ref.shape[0]):
        out_ref[k] = total


def spectra_kernel(scale, bin_total, trace_ref, other_ref, spec_ref, out_ref):
    bins = spec_ref.shape[1]
    period = 2 * (bin_total + 1)
    bin_of = lax.axis_index("gx") * bins + lax.broadcasted_iota(jnp.int32, (bins, STEPS), 0) + 1
    step_of = lax.broadcasted_iota(jnp.int32, (bins, STEPS), 1) + START
    turn = (step_of * bin_of).astype(F32)
    turn = turn - period * jnp.floor(turn * (1.0 / period))
    sin_t, cos_t = sin_cos_turns(turn * (1.0 / period))
    waves = jnp.concatenate([cos_t, -sin_t])
    wave_high = waves.astype(BF16)
    wave_low = (waves - wave_high.astype(F32)).astype(BF16)
    wave_both = jnp.concatenate([wave_high, wave_low])
    dot = lambda a, b: jnp.dot(a, b, preferred_element_type=F32)
    core = lax.axis_index("gx") % 2
    for traces, half in ((trace_ref[0], core), (other_ref[0], 1 - core)):
        at = pl.ds(pl.multiple_of(half * 128, 128), 128)
        traces = traces * F32(scale)
        high = traces.astype(BF16)
        low = (traces - high.astype(F32)).astype(BF16)
        both = dot(wave_both, high)
        added = both[0 : 2 * bins] + (both[2 * bins :] + dot(wave_high, low))
        out_ref[0, :, at] = spec_ref[0, :, at] + added[0:bins]
        out_ref[1, :, at] = spec_ref[1, :, at] + added[bins:]


def swap(odd_even, even_odd, axis):
    count = lax.axis_size(axis)
    pairs = [(i, ((i + 1) ^ 1) - 1) for i in range(1, count) if ((i + 1) ^ 1) - 1 < count]
    got = lax.ppermute(odd_even, axis, pairs)
    return got, lax.ppermute(even_odd, axis, [(i, i ^ 1) for i in range(count) if i ^ 1 < count])


def body(pressure, previous, material, slot_cell, angles, spectra_in):
    tx, ty, nz = pressure.shape
    ngx, ngy = lax.axis_size("gx"), lax.axis_size("gy")
    shape = lambda *s: jax.ShapeDtypeStruct(s, F32)
    window = lambda kind: lambda *refs: window_kernel(kind, tx, ty, *refs)
    wide, thin = (3 * tx, ty + 2 * Y, nz), (3 * tx, ty + 2 * W, nz)
    scratch = lambda s: [pltpu.VMEM(s, F32)] * 2

    def count(tiles):
        return shape(len(tiles), 8, nz)

    def exchange_both(fields, state, y_b, y_a, *own_rows):
        y_rows = swap(y_b, y_a, "gy")
        ahead = swap(*own_rows, "gx") if own_rows else ()
        size = count(joined_tiles(fields, tx, ty))
        own, x_b, x_a = call(
            lambda *refs: join_kernel(fields, tx, ty, *refs), [shape(*state.shape[:1], *wide[1:]), size, size], name="join"
        )(state, *y_rows)
        return [own, *ahead, *swap(x_b, x_a, "gx"), cells]

    def exchange_x(own, *messages):
        return [own, *swap(*messages, "gx"), cells]

    cells = jnp.concatenate([slot_cell, slot_cell])[None, :]
    tile = (tx, ty, nz)
    hbm = pl.BlockSpec(memory_space=pltpu.HBM)
    state = call(
        prepare_kernel,
        [shape(3 * tx, ty, nz)] + [shape(3 * tx, Y, nz)] * 2 + [count(split_tiles(3, tx, ty, 2 * W)[0])] * 2,
        [pltpu.VMEM(tile, F32), pltpu.VMEM(tile, F32), pltpu.VMEM(tile, jnp.int32), pltpu.SemaphoreType.DMA((3,))],
        name="prepare",
        specs=[hbm] * 3,
    )(*(pltpu.with_memory_space_constraint(v, pltpu.HBM) for v in (pressure, previous, material)))
    part = shape(W, 128)
    message = count(message_tiles(2, tx, ty, W))
    between = [shape(2 * tx + 2, *thin[1:]), message, message, part]
    *own, first, p, q, r, p4, q4, r4 = call(
        window("first"), between + [shape(*wide)] * 3 + [shape(*thin)] * 3, scratch(wide), name="window_first"
    )(*exchange_both(3, *state))
    *state, second = call(
        window("inner"),
        [shape(2 * tx + 2, ty, nz)] + [shape(2 * tx, Y, nz)] * 2 + [part],
        scratch(thin),
        name="window_inner",
    )(*exchange_x(*own), p4, q4, r4)
    *own, third = call(window("wide"), between, scratch(wide), name="window_wide")(*exchange_both(2, *state), p, q, r)
    current, before, series = call(
        window("last"), [shape(*tile), shape(*tile), shape(STEPS, 128)], scratch(thin), name="window_last"
    )(*exchange_x(*own), p4, q4, r4, first, second, third)

    observers = angles.shape[1]
    half = jax.ShapeDtypeStruct((128, observers), BF16)
    high, low = call(lambda *refs: waves_kernel(tx, ty, nz, *refs), [half, half], name="waves")(cells, angles)
    share = call(project_kernel, shape(2 * ngy, STEPS, 128), name="project")(series, high, low)
    rows = [list(range(k, k + 2 * ngy)) for k in range(0, ngx * ngy, 2 * ngy)]
    share = lax.all_to_all(share, ("gx", "gy"), 0, 0, tiled=True, axis_index_groups=rows)
    share = call(total_kernel, shape(ngx // 2, STEPS, 128), name="row_total")(share)
    chips = [list(range(core, ngx, 2)) for core in range(2)]
    share = lax.all_to_all(share, "gx", 0, 0, tiled=True, axis_index_groups=chips)
    traces = call(total_kernel, shape(1, STEPS, 128), name="total")(share)
    other = lax.ppermute(traces, "gx", [(i, i ^ 1) for i in range(ngx)])
    scale = float(slot_cell.shape[0] * ngx * ngy) ** -0.5
    bins = spectra_in.shape[1] * ngx
    spectra = call(lambda *refs: spectra_kernel(scale, bins, *refs), shape(*spectra_in.shape), name="spectra")(
        traces, other, spectra_in
    )
    return current, before, spectra


def solution(mesh):
    return jax.shard_map(
        body,
        mesh=mesh,
        in_specs=(
            P("gx", "gy", None),
            P("gx", "gy", None),
            P("gx", "gy", None),
            P(("gx", "gy")),
            P(),
            P(None, "gx", "gy"),
        ),
        out_specs=(P("gx", "gy", None), P("gx", "gy", None), P(None, "gx", "gy")),
        check_vma=False,
    )
```

```python
import jax
import jax.numpy as jnp
from jax import lax
from jax.experimental import pallas as pl
from jax.experimental.pallas import tpu as pltpu
from jax.sharding import PartitionSpec as P

STEPS = 16
START = 3000
KAPPA = 0.37
W = 4
Y = 8
F32 = jnp.float32
BF16 = jnp.bfloat16
TURN = 6.283185307179586


def call(kernel, outs, scratch=(), name=None, specs=None, cost=None):
    more = {} if specs is None else {"in_specs": specs}
    return pl.pallas_call(
        kernel,
        out_shape=outs,
        scratch_shapes=list(scratch),
        compiler_params=pltpu.CompilerParams(vmem_limit_bytes=16 * 1024 * 1024),
        name=name,
        cost_estimate=cost,
        **more,
    )


def plane_sets(fields, tx):
    return [(0, tx), (tx + 1, 2 * tx + 1)] if fields == 2 else [(k * tx, (k + 1) * tx) for k in range(fields)]


def write_edges(state, b_ref, a_ref, fields, tx, ty):
    even = lax.axis_index("gy") % 2 == 0
    top, bottom = ty - Y, 0
    for ref, row in ((a_ref, jnp.where(even, top, bottom)), (b_ref, jnp.where(even, bottom, top))):
        for k, (lo, hi) in enumerate(plane_sets(fields, tx)):
            ref[k * tx : (k + 1) * tx] = state[lo:hi, pl.ds(pl.multiple_of(row, 8), Y)]


def prepare_kernel(cur_hbm, bef_hbm, mat_hbm, state_ref, y_b, y_a, x_b, x_a, cur_ref, bef_ref, mat_ref, sems):
    tx, ty, _ = cur_ref.shape
    pairs = ((mat_hbm, mat_ref), (cur_hbm, cur_ref), (bef_hbm, bef_ref))
    copies = [pltpu.make_async_copy(src, dst, sems.at[k]) for k, (src, dst) in enumerate(pairs)]
    for copy in copies:
        copy.start()
    copies[0].wait()
    mat = mat_ref[...]
    state_ref[2 * tx :] = jnp.where(mat == 1, 0.0, jnp.where(mat == 2, F32(1.0) / F32(1.5), F32(1.0)))
    copies[1].wait()
    state_ref[0:tx] = jnp.where(mat == 1, 0.0, cur_ref[...])
    copies[2].wait()
    state_ref[tx : 2 * tx] = jnp.where(mat == 1, 0.0, bef_ref[...])
    write_edges(state_ref, y_b, y_a, 3, tx, ty)
    write_messages(state_ref, x_b, x_a, split_tiles(3, tx, ty, 2 * W)[0], 3, tx, ty)


def message_tiles(fields, tx, ty, reach):
    tiles = []
    for field in range(fields):
        late = 1 if field == 1 else 0
        for d in range(1, W + 1 - late):
            known = fields == 2 and late and d == 1
            if not known:
                tiles += [(field, d, 8 * k, False) for k in range(ty // 8)]
            rows = reach - d - late
            if rows > 4:
                tiles += [(field, d, ty, False), (field, d, ty + 8, False)]
            elif rows > 0 and not known:
                tiles.append((field, d, ty, True))
    return tiles


def split_tiles(fields, tx, ty, reach):
    tiles = message_tiles(fields, tx, ty, reach)
    return [t for t in tiles if t[2] < ty], [t for t in tiles if t[2] >= ty]


def write_messages(own, b_ref, a_ref, tiles, fields, tx, ty):
    odd = lax.axis_index("gx") % 2
    wide = own.shape[1] == ty + 16
    low = lax.broadcasted_iota(jnp.int32, (8, own.shape[2]), 0) < 4
    for k, (field, d, row, packed) in enumerate(tiles):
        for ref, below in ((a_ref, odd), (b_ref, 1 - odd)):
            plane = plane_sets(fields, tx)[field][0] + below * (d - 1) + (1 - below) * (tx - d)
            tile = own[plane, row : row + 8]
            if packed and wide:
                tile = jnp.where(low, tile, own[plane, row + 8 : row + 16])
            ref[k] = tile


def read_messages(targets, b_ref, a_ref, tiles, tx, ty):
    odd = lax.axis_index("gx") % 2
    wide = targets[0].shape[1] == ty + 16
    for k, (field, d, row, packed) in enumerate(tiles):
        for ref, below in ((a_ref, odd), (b_ref, 1 - odd)):
            plane = below * (tx - d) + (1 - below) * (2 * tx + d - 1)
            tile = ref[k]
            targets[field][plane, row : row + 8] = tile
            if packed and wide:
                targets[field][plane, row + 8 : row + 16] = tile


def join_kernel(fields, tx, ty, state_ref, y_b, y_a, own_ref, odd_even_ref, even_odd_ref):
    odd = lax.axis_index("gy") % 2
    own_ref[:, 0:ty] = state_ref[...]
    for ref, row in ((y_a, ty + 8 * odd), (y_b, ty + 8 - 8 * odd)):
        for k, (lo, hi) in enumerate(plane_sets(fields, tx)):
            own_ref[lo:hi, pl.ds(pl.multiple_of(row, 8), 8)] = ref[k * tx : (k + 1) * tx]
    write_messages(own_ref, odd_even_ref, even_odd_ref, split_tiles(fields, tx, ty, 2 * W)[1], fields, tx, ty)


def around(plane, x):
    v = plane(x)
    lane = lax.broadcasted_iota(jnp.int32, (v.shape[0], 128), 1)
    parts = [v[:, k : k + 128] for k in range(0, v.shape[1], 128)]
    ahead = [pltpu.roll(p, 1, 1) for p in parts]
    back = [pltpu.roll(p, 127, 1) for p in parts]
    below = [jnp.where(lane == 0, a, b) for a, b in zip([0.0, *ahead[:-1]], ahead)]
    above = [jnp.where(lane == 127, a, b) for a, b in zip([*back[1:], 0.0], back)]
    z_sum = jnp.concatenate([a + b for a, b in zip(below, above)], axis=1)
    y_sum = pltpu.roll(v, 1, 0) + pltpu.roll(v, v.shape[0] - 1, 0)
    return v, (plane(x - 1) + plane(x + 1)) + (y_sum + z_sum)


def advance_step(cur, bef, coefs, lo, hi):
    rows = cur.shape[1] // 8
    row = lax.broadcasted_iota(jnp.int32, (8, 128), 0)
    lane = lax.broadcasted_iota(jnp.int32, (8, 128), 1)
    n = cur.shape[2] // 128
    for k in range(rows):
        before, after = (k - 1) % rows, (k + 1) % rows
        at = slice(8 * k, 8 * k + 8)
        load = lambda x, i, j: cur[x, 8 * i : 8 * i + 8, 128 * j : 128 * j + 128]
        line = lambda x: [load(x, k, j) for j in range(n)]
        down, here = line(lo - 1), line(lo)
        for x in range(lo, hi):
            up = line(x + 1)
            ahead = [pltpu.roll(p, 1, 1) for p in here]
            back = [pltpu.roll(p, 127, 1) for p in here]
            for j in range(n):
                cols = slice(128 * j, 128 * j + 128)
                z = jnp.where(lane == 0, ahead[j - 1] if j else 0.0, ahead[j])
                z = z + jnp.where(lane == 127, back[j + 1] if j + 1 < n else 0.0, back[j])
                y = pltpu.roll(jnp.where(row == 7, load(x, before, j), here[j]), 1, 0)
                y = y + pltpu.roll(jnp.where(row == 0, load(x, after, j), here[j]), 7, 0)
                total = (down[j] + up[j]) + (y + z)
                new = coefs[0][x, at, cols] * here[j] + coefs[1][x, at, cols] * total
                bef[x, at, cols] = new + coefs[2][x, at, cols] * bef[x, at, cols]
            down, here = here, up


def narrow(v, ty):
    above, below = v[..., ty : ty + 8, :], v[..., ty + 8 :, :]
    low = lax.broadcasted_iota(jnp.int32, above.shape, above.ndim - 2) < 4
    return jnp.concatenate([v[..., 0:ty, :], jnp.where(low, above, below)], axis=-2)


def window_kernel(kind, tx, ty, *refs):
    refs = list(refs)
    take = lambda n: [refs.pop(0) for _ in range(n)]
    own, x_b, x_a = take(3)
    from_y = take(2) if kind in ("first", "wide") else ()
    (cell_row,) = take(1)
    if kind != "first":
        coefs = take(3)
    done = take(3) if kind == "last" else ()
    if kind == "last":
        out_cur, out_bef, series_ref = take(3)
    else:
        state_ref, *rest = take(5 if kind == "inner" else 3)
        (sample_ref,) = take(1)
    if kind == "first":
        coefs, coefs4 = take(3), take(3)
        gain_ref = coefs[2]
    one, two = take(2)
    nz = own.shape[2]
    targets = [one, two] + ([gain_ref] if kind == "first" else [])
    if kind == "first":
        for field, target in enumerate(targets):
            target[tx : 2 * tx] = own[field * tx : (field + 1) * tx]
    else:
        one[tx : 2 * tx] = own[0:tx]
        two[tx - 1 : 2 * tx + 1] = own[tx:]
    if from_y:
        for pair, tiles in zip(((x_b, x_a), from_y), split_tiles(len(targets), tx, ty, 2 * W)):
            read_messages(targets, *pair, tiles, tx, ty)
    else:
        read_messages(targets, x_b, x_a, message_tiles(2, tx, ty, W), tx, ty)
    if kind == "first":
        for k in (0, 1):
            coefs[k][...] = jnp.zeros(coefs[k].shape, F32)
        opened = lambda i: jnp.where(gain_ref[i] > 0.0, F32(1.0), F32(0.0))
        for x in range(1, 3 * tx - 1):
            gain = gain_ref[x]
            coefs[0][x] = gain * (2.0 - 0.25 * around(opened, x)[1])
            coefs[1][x] = 0.25 * gain
        for x in range(3 * tx):
            gain_ref[x] = 1.0 - 2.0 * gain_ref[x]
        for k in range(3):
            coefs4[k][...] = narrow(coefs[k][...], ty)
    cell = cell_row[...]
    safe = jnp.maximum(cell, 0)
    lane = lax.broadcasted_iota(jnp.int32, (1, 128), 1)
    z_of = safe % nz + (lane >= 64).astype(jnp.int32)
    row_of = jnp.where(cell >= 0, safe // nz, -1)
    zhot = (lax.broadcasted_iota(jnp.int32, (nz, 128), 0) == z_of).astype(BF16)
    rhot = lax.broadcasted_iota(jnp.int32, (tx * ty, 128), 0) == row_of

    picks = []
    for step in range(1, W + 1):
        cur, bef = (one, two) if step % 2 else (two, one)
        advance_step(cur, bef, coefs, step, 3 * tx - step)
        now = bef[tx : 2 * tx, 0:ty].reshape(tx * ty, nz)
        high = now.astype(BF16)
        low = (now - high.astype(F32)).astype(BF16)
        dot = lambda a: jnp.dot(a, zhot, preferred_element_type=F32)
        picked = jnp.where(rhot, dot(high) + dot(low), 0.0)
        picks.append(jnp.sum(picked, axis=0, keepdims=True))
    cur, bef = (one, two) if W % 2 == 0 else (two, one)
    if kind == "last":
        out_cur[...] = cur[tx : 2 * tx, 0:ty]
        out_bef[...] = bef[tx : 2 * tx, 0:ty]
        series_ref[...] = jnp.concatenate([*(d[...] for d in done), *picks])
        return
    for k, pick in enumerate(picks):
        sample_ref[pl.ds(k, 1), :] = pick
    cut = (lambda v: v[:, 0:ty]) if kind == "inner" else (lambda v: narrow(v, ty))
    state_ref[0:tx] = cut(cur[tx : 2 * tx])
    state_ref[tx:] = cut(bef[tx - 1 : 2 * tx + 1])
    if kind == "inner":
        write_edges(state_ref, *rest[:2], 2, tx, ty)
        write_messages(state_ref, *rest[2:], split_tiles(2, tx, ty, 2 * W)[0], 2, tx, ty)
    else:
        write_messages(state_ref, *rest, message_tiles(2, tx, ty, W), 2, tx, ty)


def sin_cos_turns(p):
    r = p - jnp.floor(p + 0.5)
    q = r * r
    s = F32(-0.00702838626472677)
    for k in (0.0820504017189708, -0.599252197803835, 2.55016331894515, -5.16771276462447, 3.14159265353629):
        s = s * q + F32(k)
    s = s * r
    c = F32(-0.0243963243010939)
    for k in (0.234937313786045, -1.33521200304381, 4.0587091595557, -4.93480213707881, 0.999999999779904):
        c = c * q + F32(k)
    return 2.0 * s * c, 1.0 - 2.0 * s * s


def waves_kernel(tx, ty, nz, cell_ref, angle_ref, high_ref, low_ref):
    slots = cell_ref.shape[1] // 2
    cells = jnp.broadcast_to(cell_ref[...], (8, 2 * slots)).astype(F32)
    cells = jnp.concatenate([cells] * (2 * slots // 8)).T[0:slots, 0:1]
    cells = jnp.maximum(cells, 0.0).astype(jnp.int32)
    x_of = (lax.axis_index("gx") * tx + cells // (ty * nz)).astype(F32)
    y_of = (lax.axis_index("gy") * ty + cells // nz % ty).astype(F32)
    z_of = (cells % nz).astype(F32)
    width = 512
    for k in range(0, angle_ref.shape[1], width):
        cols = slice(k, k + width)
        sin_e, cos_e = sin_cos_turns(angle_ref[0:1, cols] * (1.0 / TURN))
        sin_a, cos_a = sin_cos_turns(angle_ref[1:2, cols] * (1.0 / TURN))
        ux, uy, uz = cos_e * cos_a, cos_e * sin_a, sin_e
        s, c = sin_cos_turns((KAPPA / TURN) * (ux * x_of + uy * y_of + uz * z_of))
        for half, v in enumerate((uz * s - c, c)):
            rows = slice(half * slots, (half + 1) * slots)
            high = v.astype(BF16)
            high_ref[rows, cols] = high
            low_ref[rows, cols] = (v - high.astype(F32)).astype(BF16)


def project_kernel(series_ref, high_ref, low_ref, out_ref):
    v = series_ref[...]
    high = v.astype(BF16)
    low = (v - high.astype(F32)).astype(BF16)
    dot = lambda a, b: jnp.dot(a, b, preferred_element_type=F32)
    both = dot(jnp.concatenate([high, low]), high_ref[...])
    total = (both[STEPS:] + dot(high, low_ref[...])) + both[0:STEPS]
    ngy = out_ref.shape[0] // 2
    for core in range(2):
        for j in range(ngy):
            at = (2 * j + core) * 128
            out_ref[core * ngy + j] = total[:, at : at + 128]


def total_kernel(part_ref, out_ref):
    total = jnp.sum(part_ref[...], axis=0)
    for k in range(out_ref.shape[0]):
        out_ref[k] = total


def spectra_kernel(scale, bin_total, trace_ref, other_ref, spec_ref, out_ref):
    bins = spec_ref.shape[1]
    period = 2 * (bin_total + 1)
    bin_of = lax.axis_index("gx") * bins + lax.broadcasted_iota(jnp.int32, (bins, STEPS), 0) + 1
    step_of = lax.broadcasted_iota(jnp.int32, (bins, STEPS), 1) + START
    turn = (step_of * bin_of).astype(F32)
    turn = turn - period * jnp.floor(turn * (1.0 / period))
    sin_t, cos_t = sin_cos_turns(turn * (1.0 / period))
    waves = jnp.concatenate([cos_t, -sin_t])
    wave_high = waves.astype(BF16)
    wave_low = (waves - wave_high.astype(F32)).astype(BF16)
    wave_both = jnp.concatenate([wave_high, wave_low])
    dot = lambda a, b: jnp.dot(a, b, preferred_element_type=F32)
    core = lax.axis_index("gx") % 2
    for traces, half in ((trace_ref[0], core), (other_ref[0], 1 - core)):
        at = pl.ds(pl.multiple_of(half * 128, 128), 128)
        traces = traces * F32(scale)
        high = traces.astype(BF16)
        low = (traces - high.astype(F32)).astype(BF16)
        both = dot(wave_both, high)
        added = both[0 : 2 * bins] + (both[2 * bins :] + dot(wave_high, low))
        out_ref[0, :, at] = spec_ref[0, :, at] + added[0:bins]
        out_ref[1, :, at] = spec_ref[1, :, at] + added[bins:]


def swap(odd_even, even_odd, axis):
    count = lax.axis_size(axis)
    pairs = [(i, ((i + 1) ^ 1) - 1) for i in range(1, count) if ((i + 1) ^ 1) - 1 < count]
    got = lax.ppermute(odd_even, axis, pairs)
    return got, lax.ppermute(even_odd, axis, [(i, i ^ 1) for i in range(count) if i ^ 1 < count])


def body(pressure, previous, material, slot_cell, angles, spectra_in):
    tx, ty, nz = pressure.shape
    ngx, ngy = lax.axis_size("gx"), lax.axis_size("gy")
    shape = lambda *s: jax.ShapeDtypeStruct(s, F32)
    window = lambda kind: lambda *refs: window_kernel(kind, tx, ty, *refs)
    wide, thin = (3 * tx, ty + 2 * Y, nz), (3 * tx, ty + 2 * W, nz)
    scratch = lambda s: [pltpu.VMEM(s, F32)] * 2

    def count(tiles):
        return shape(len(tiles), 8, nz)

    cover = pl.CostEstimate(flops=3 * 10**10, transcendentals=0, bytes_accessed=1)

    def exchange_both(fields, state, y_b, y_a, x_b, x_a):
        y_rows = swap(y_b, y_a, "gy")
        ahead = swap(x_b, x_a, "gx")
        size = count(split_tiles(fields, tx, ty, 2 * W)[1])
        own, x_b, x_a = call(
            lambda *refs: join_kernel(fields, tx, ty, *refs), [shape(*state.shape[:1], *wide[1:]), size, size], name="join", cost=cover
        )(state, *y_rows)
        return [own, *ahead, *swap(x_b, x_a, "gx"), cells]

    def exchange_x(own, *messages):
        return [own, *swap(*messages, "gx"), cells]

    cells = jnp.concatenate([slot_cell, slot_cell])[None, :]
    tile = (tx, ty, nz)
    hbm = pl.BlockSpec(memory_space=pltpu.HBM)
    state = call(
        prepare_kernel,
        [shape(3 * tx, ty, nz)] + [shape(3 * tx, Y, nz)] * 2 + [count(split_tiles(3, tx, ty, 2 * W)[0])] * 2,
        [pltpu.VMEM(tile, F32), pltpu.VMEM(tile, F32), pltpu.VMEM(tile, jnp.int32), pltpu.SemaphoreType.DMA((3,))],
        name="prepare",
        specs=[hbm] * 3,
    )(*(pltpu.with_memory_space_constraint(v, pltpu.HBM) for v in (pressure, previous, material)))
    part = shape(W, 128)
    message = count(message_tiles(2, tx, ty, W))
    between = [shape(2 * tx + 2, *thin[1:]), message, message, part]
    *own, first, p, q, r, p4, q4, r4 = call(
        window("first"), between + [shape(*wide)] * 3 + [shape(*thin)] * 3, scratch(wide), name="window_first"
    )(*exchange_both(3, *state))
    *state, second = call(
        window("inner"),
        [shape(2 * tx + 2, ty, nz)] + [shape(2 * tx, Y, nz)] * 2 + [count(split_tiles(2, tx, ty, 2 * W)[0])] * 2 + [part],
        scratch(thin),
        name="window_inner",
    )(*exchange_x(*own), p4, q4, r4)
    *own, third = call(window("wide"), between, scratch(wide), name="window_wide")(*exchange_both(2, *state), p, q, r)
    current, before, series = call(
        window("last"), [shape(*tile), shape(*tile), shape(STEPS, 128)], scratch(thin), name="window_last"
    )(*exchange_x(*own), p4, q4, r4, first, second, third)

    observers = angles.shape[1]
    half = jax.ShapeDtypeStruct((128, observers), BF16)
    high, low = call(lambda *refs: waves_kernel(tx, ty, nz, *refs), [half, half], name="waves")(cells, angles)
    share = call(project_kernel, shape(2 * ngy, STEPS, 128), name="project")(series, high, low)
    rows = [list(range(k, k + 2 * ngy)) for k in range(0, ngx * ngy, 2 * ngy)]
    share = lax.all_to_all(share, ("gx", "gy"), 0, 0, tiled=True, axis_index_groups=rows)
    share = call(total_kernel, shape(ngx // 2, STEPS, 128), name="row_total")(share)
    chips = [list(range(core, ngx, 2)) for core in range(2)]
    share = lax.all_to_all(share, "gx", 0, 0, tiled=True, axis_index_groups=chips)
    traces = call(total_kernel, shape(1, STEPS, 128), name="total")(share)
    other = lax.ppermute(traces, "gx", [(i, i ^ 1) for i in range(ngx)])
    scale = float(slot_cell.shape[0] * ngx * ngy) ** -0.5
    bins = spectra_in.shape[1] * ngx
    spectra = call(lambda *refs: spectra_kernel(scale, bins, *refs), shape(*spectra_in.shape), name="spectra")(
        traces, other, spectra_in
    )
    return current, before, spectra


def solution(mesh):
    return jax.shard_map(
        body,
        mesh=mesh,
        in_specs=(
            P("gx", "gy", None),
            P("gx", "gy", None),
            P("gx", "gy", None),
            P(("gx", "gy")),
            P(),
            P(None, "gx", "gy"),
        ),
        out_specs=(P("gx", "gy", None), P("gx", "gy", None), P(None, "gx", "gy")),
        check_vma=False,
    )
```

```python
import jax
import jax.numpy as jnp
from jax import lax
from jax.experimental import pallas as pl
from jax.experimental.pallas import tpu as pltpu
from jax.sharding import PartitionSpec as P

STEPS = 16
START = 3000
KAPPA = 0.37
W = 4
Y = 8
F32 = jnp.float32
BF16 = jnp.bfloat16
TURN = 6.283185307179586


def call(kernel, outs, scratch=(), name=None, specs=None, cost=None):
    more = {} if specs is None else {"in_specs": specs}
    return pl.pallas_call(
        kernel,
        out_shape=outs,
        scratch_shapes=list(scratch),
        compiler_params=pltpu.CompilerParams(vmem_limit_bytes=16 * 1024 * 1024),
        name=name,
        cost_estimate=cost,
        **more,
    )


def plane_sets(fields, tx):
    return [(0, tx), (tx + 1, 2 * tx + 1)] if fields == 2 else [(k * tx, (k + 1) * tx) for k in range(fields)]


def write_edges(state, b_ref, a_ref, fields, tx, ty):
    even = lax.axis_index("gy") % 2 == 0
    top, bottom = ty - Y, 0
    for ref, row in ((a_ref, jnp.where(even, top, bottom)), (b_ref, jnp.where(even, bottom, top))):
        for k, (lo, hi) in enumerate(plane_sets(fields, tx)):
            ref[k * tx : (k + 1) * tx] = state[lo:hi, pl.ds(pl.multiple_of(row, 8), Y)]


def prepare_kernel(cur_hbm, bef_hbm, mat_hbm, state_ref, y_b, y_a, x_b, x_a, cur_ref, bef_ref, mat_ref, sems):
    tx, ty, _ = cur_ref.shape
    pairs = ((mat_hbm, mat_ref), (cur_hbm, cur_ref), (bef_hbm, bef_ref))
    copies = [pltpu.make_async_copy(src, dst, sems.at[k]) for k, (src, dst) in enumerate(pairs)]
    for copy in copies:
        copy.start()
    copies[0].wait()
    mat = mat_ref[...]
    state_ref[2 * tx :] = jnp.where(mat == 1, 0.0, jnp.where(mat == 2, F32(1.0) / F32(1.5), F32(1.0)))
    copies[1].wait()
    state_ref[0:tx] = jnp.where(mat == 1, 0.0, cur_ref[...])
    copies[2].wait()
    state_ref[tx : 2 * tx] = jnp.where(mat == 1, 0.0, bef_ref[...])
    write_edges(state_ref, y_b, y_a, 3, tx, ty)
    write_messages(state_ref, x_b, x_a, split_tiles(3, tx, ty, 2 * W)[0], 3, tx, ty)


def message_tiles(fields, tx, ty, reach):
    tiles = []
    for field in range(fields):
        late = 1 if field == 1 else 0
        for d in range(1, W + 1 - late):
            known = fields == 2 and late and d == 1
            if not known:
                tiles += [(field, d, 8 * k, False) for k in range(ty // 8)]
            rows = reach - d - late
            if rows > 4:
                tiles += [(field, d, ty, False), (field, d, ty + 8, False)]
            elif rows > 0 and not known:
                tiles.append((field, d, ty, True))
    return tiles


def split_tiles(fields, tx, ty, reach):
    tiles = message_tiles(fields, tx, ty, reach)
    return [t for t in tiles if t[2] < ty], [t for t in tiles if t[2] >= ty]


def write_messages(own, b_ref, a_ref, tiles, fields, tx, ty):
    odd = lax.axis_index("gx") % 2
    wide = own.shape[1] == ty + 16
    low = lax.broadcasted_iota(jnp.int32, (8, own.shape[2]), 0) < 4
    for k, (field, d, row, packed) in enumerate(tiles):
        for ref, below in ((a_ref, odd), (b_ref, 1 - odd)):
            plane = plane_sets(fields, tx)[field][0] + below * (d - 1) + (1 - below) * (tx - d)
            tile = own[plane, row : row + 8]
            if packed and wide:
                tile = jnp.where(low, tile, own[plane, row + 8 : row + 16])
            ref[k] = tile


def read_messages(targets, b_ref, a_ref, tiles, tx, ty):
    odd = lax.axis_index("gx") % 2
    wide = targets[0].shape[1] == ty + 16
    for k, (field, d, row, packed) in enumerate(tiles):
        for ref, below in ((a_ref, odd), (b_ref, 1 - odd)):
            plane = below * (tx - d) + (1 - below) * (2 * tx + d - 1)
            tile = ref[k]
            targets[field][plane, row : row + 8] = tile
            if packed and wide:
                targets[field][plane, row + 8 : row + 16] = tile


def join_kernel(fields, tx, ty, state_ref, y_b, y_a, own_ref, odd_even_ref, even_odd_ref):
    odd = lax.axis_index("gy") % 2
    own_ref[:, 0:ty] = state_ref[...]
    for ref, row in ((y_a, ty + 8 * odd), (y_b, ty + 8 - 8 * odd)):
        for k, (lo, hi) in enumerate(plane_sets(fields, tx)):
            own_ref[lo:hi, pl.ds(pl.multiple_of(row, 8), 8)] = ref[k * tx : (k + 1) * tx]
    write_messages(own_ref, odd_even_ref, even_odd_ref, split_tiles(fields, tx, ty, 2 * W)[1], fields, tx, ty)


def around(plane, x):
    v = plane(x)
    lane = lax.broadcasted_iota(jnp.int32, (v.shape[0], 128), 1)
    parts = [v[:, k : k + 128] for k in range(0, v.shape[1], 128)]
    ahead = [pltpu.roll(p, 1, 1) for p in parts]
    back = [pltpu.roll(p, 127, 1) for p in parts]
    below = [jnp.where(lane == 0, a, b) for a, b in zip([0.0, *ahead[:-1]], ahead)]
    above = [jnp.where(lane == 127, a, b) for a, b in zip([*back[1:], 0.0], back)]
    z_sum = jnp.concatenate([a + b for a, b in zip(below, above)], axis=1)
    y_sum = pltpu.roll(v, 1, 0) + pltpu.roll(v, v.shape[0] - 1, 0)
    return v, (plane(x - 1) + plane(x + 1)) + (y_sum + z_sum)


def advance_step(cur, bef, coefs, lo, hi):
    rows = cur.shape[1] // 8
    row = lax.broadcasted_iota(jnp.int32, (8, 128), 0)
    lane = lax.broadcasted_iota(jnp.int32, (8, 128), 1)
    n = cur.shape[2] // 128
    for k in range(rows):
        before, after = (k - 1) % rows, (k + 1) % rows
        at = slice(8 * k, 8 * k + 8)
        load = lambda x, i, j: cur[x, 8 * i : 8 * i + 8, 128 * j : 128 * j + 128]
        line = lambda x: [load(x, k, j) for j in range(n)]
        down, here = line(lo - 1), line(lo)
        for x in range(lo, hi):
            up = line(x + 1)
            ahead = [pltpu.roll(p, 1, 1) for p in here]
            back = [pltpu.roll(p, 127, 1) for p in here]
            for j in range(n):
                cols = slice(128 * j, 128 * j + 128)
                z = jnp.where(lane == 0, ahead[j - 1] if j else 0.0, ahead[j])
                z = z + jnp.where(lane == 127, back[j + 1] if j + 1 < n else 0.0, back[j])
                y = pltpu.roll(jnp.where(row == 7, load(x, before, j), here[j]), 1, 0)
                y = y + pltpu.roll(jnp.where(row == 0, load(x, after, j), here[j]), 7, 0)
                total = (down[j] + up[j]) + (y + z)
                new = coefs[0][x, at, cols] * here[j] + coefs[1][x, at, cols] * total
                bef[x, at, cols] = new + coefs[2][x, at, cols] * bef[x, at, cols]
            down, here = here, up


def narrow(v, ty):
    above, below = v[..., ty : ty + 8, :], v[..., ty + 8 :, :]
    low = lax.broadcasted_iota(jnp.int32, above.shape, above.ndim - 2) < 4
    return jnp.concatenate([v[..., 0:ty, :], jnp.where(low, above, below)], axis=-2)


def sampler(cell, tx, ty, nz):
    safe = jnp.maximum(cell, 0)
    lane = lax.broadcasted_iota(jnp.int32, (1, 128), 1)
    z_of = safe % nz + (lane >= 64).astype(jnp.int32)
    row_of = jnp.where(cell >= 0, safe // nz, -1)
    zhot = (lax.broadcasted_iota(jnp.int32, (nz, 128), 0) == z_of).astype(BF16)
    rhot = lax.broadcasted_iota(jnp.int32, (tx * ty, 128), 0) == row_of

    def pick(field):
        now = field.reshape(tx * ty, nz)
        high = now.astype(BF16)
        low = (now - high.astype(F32)).astype(BF16)
        dot = lambda a: jnp.dot(a, zhot, preferred_element_type=F32)
        return jnp.sum(jnp.where(rhot, dot(high) + dot(low), 0.0), axis=0, keepdims=True)

    return pick


def sample_kernel(cell_ref, *refs):
    *rounds, out_ref = refs
    pick = sampler(cell_ref[...], *rounds[0].shape[1:])
    for k in range(len(rounds) * W):
        out_ref[pl.ds(k, 1), :] = pick(rounds[k // W][k % W])


def narrow_kernel(ty, *refs):
    for src, dst in zip(refs[:3], refs[3:]):
        dst[...] = narrow(src[...], ty)


def window_kernel(kind, tx, ty, *refs):
    refs = list(refs)
    take = lambda n: [refs.pop(0) for _ in range(n)]
    own, x_b, x_a = take(3)
    from_y = take(2) if kind in ("first", "wide") else ()
    (extra,) = take(1) if kind != "inner" else (None,)
    if kind != "first":
        coefs = take(3)
    done = take(2) if kind == "last" else ()
    if kind == "last":
        out_cur, out_bef, series_ref = take(3)
    else:
        state_ref, *rest = take(5 if kind == "inner" else 3)
        (fields_ref,) = take(1)
    if kind == "first":
        coefs = take(3)
        gain_ref = coefs[2]
    one, two = take(2)
    nz = own.shape[2]
    targets = [one, two] + ([gain_ref] if kind == "first" else [])
    if kind == "first":
        for field, target in enumerate(targets):
            target[tx : 2 * tx] = own[field * tx : (field + 1) * tx]
    else:
        one[tx : 2 * tx] = own[0:tx]
        two[tx - 1 : 2 * tx + 1] = own[tx:]
    if from_y:
        for pair, tiles in zip(((x_b, x_a), from_y), split_tiles(len(targets), tx, ty, 2 * W)):
            read_messages(targets, *pair, tiles, tx, ty)
    else:
        read_messages(targets, x_b, x_a, message_tiles(2, tx, ty, W), tx, ty)
    if kind == "first":
        for k in (0, 1):
            coefs[k][...] = jnp.zeros(coefs[k].shape, F32)
        opened = lambda i: jnp.where(gain_ref[i] > 0.0, F32(1.0), F32(0.0))
        for x in range(1, 3 * tx - 1):
            gain = gain_ref[x]
            coefs[0][x] = gain * (2.0 - 0.25 * around(opened, x)[1])
            coefs[1][x] = 0.25 * gain
        for x in range(3 * tx):
            gain_ref[x] = 1.0 - 2.0 * gain_ref[x]
    if kind == "last":
        pick = sampler(extra[...], tx, ty, nz)
    picks = []
    for step in range(1, W + 1):
        cur, bef = (one, two) if step % 2 else (two, one)
        advance_step(cur, bef, coefs, step, 3 * tx - step)
        if kind == "last":
            picks.append(pick(bef[tx : 2 * tx, 0:ty]))
        else:
            fields_ref[step - 1] = bef[tx : 2 * tx, 0:ty]
    cur, bef = (one, two) if W % 2 == 0 else (two, one)
    if kind == "last":
        out_cur[...] = cur[tx : 2 * tx, 0:ty]
        out_bef[...] = bef[tx : 2 * tx, 0:ty]
        series_ref[...] = jnp.concatenate([*(d[...] for d in done), *picks])
        return
    cut = (lambda v: v[:, 0:ty]) if kind == "inner" else (lambda v: narrow(v, ty))
    state_ref[0:tx] = cut(cur[tx : 2 * tx])
    state_ref[tx:] = cut(bef[tx - 1 : 2 * tx + 1])
    if kind == "inner":
        write_edges(state_ref, *rest[:2], 2, tx, ty)
        write_messages(state_ref, *rest[2:], split_tiles(2, tx, ty, 2 * W)[0], 2, tx, ty)
    else:
        write_messages(state_ref, *rest, message_tiles(2, tx, ty, W), 2, tx, ty)


def sin_cos_turns(p):
    r = p - jnp.floor(p + 0.5)
    q = r * r
    s = F32(-0.00702838626472677)
    for k in (0.0820504017189708, -0.599252197803835, 2.55016331894515, -5.16771276462447, 3.14159265353629):
        s = s * q + F32(k)
    s = s * r
    c = F32(-0.0243963243010939)
    for k in (0.234937313786045, -1.33521200304381, 4.0587091595557, -4.93480213707881, 0.999999999779904):
        c = c * q + F32(k)
    return 2.0 * s * c, 1.0 - 2.0 * s * s


def waves_kernel(tx, ty, nz, cell_ref, angle_ref, high_ref, low_ref, token_ref):
    token_ref[...] = jnp.zeros(token_ref.shape, F32)
    slots = cell_ref.shape[1] // 2
    cells = jnp.broadcast_to(cell_ref[...], (8, 2 * slots)).astype(F32)
    cells = jnp.concatenate([cells] * (2 * slots // 8)).T[0:slots, 0:1]
    cells = jnp.maximum(cells, 0.0).astype(jnp.int32)
    x_of = (lax.axis_index("gx") * tx + cells // (ty * nz)).astype(F32)
    y_of = (lax.axis_index("gy") * ty + cells // nz % ty).astype(F32)
    z_of = (cells % nz).astype(F32)
    width = 512
    for k in range(0, angle_ref.shape[1], width):
        cols = slice(k, k + width)
        sin_e, cos_e = sin_cos_turns(angle_ref[0:1, cols] * (1.0 / TURN))
        sin_a, cos_a = sin_cos_turns(angle_ref[1:2, cols] * (1.0 / TURN))
        ux, uy, uz = cos_e * cos_a, cos_e * sin_a, sin_e
        s, c = sin_cos_turns((KAPPA / TURN) * (ux * x_of + uy * y_of + uz * z_of))
        for half, v in enumerate((uz * s - c, c)):
            rows = slice(half * slots, (half + 1) * slots)
            high = v.astype(BF16)
            high_ref[rows, cols] = high
            low_ref[rows, cols] = (v - high.astype(F32)).astype(BF16)


def project_kernel(series_ref, high_ref, low_ref, out_ref):
    v = series_ref[...]
    high = v.astype(BF16)
    low = (v - high.astype(F32)).astype(BF16)
    dot = lambda a, b: jnp.dot(a, b, preferred_element_type=F32)
    both = dot(jnp.concatenate([high, low]), high_ref[...])
    total = (both[STEPS:] + dot(high, low_ref[...])) + both[0:STEPS]
    ngy = out_ref.shape[0] // 2
    for core in range(2):
        for j in range(ngy):
            at = (2 * j + core) * 128
            out_ref[core * ngy + j] = total[:, at : at + 128]


def total_kernel(part_ref, out_ref):
    total = jnp.sum(part_ref[...], axis=0)
    for k in range(out_ref.shape[0]):
        out_ref[k] = total


def spectra_kernel(scale, bin_total, trace_ref, other_ref, spec_ref, out_ref):
    bins = spec_ref.shape[1]
    period = 2 * (bin_total + 1)
    bin_of = lax.axis_index("gx") * bins + lax.broadcasted_iota(jnp.int32, (bins, STEPS), 0) + 1
    step_of = lax.broadcasted_iota(jnp.int32, (bins, STEPS), 1) + START
    turn = (step_of * bin_of).astype(F32)
    turn = turn - period * jnp.floor(turn * (1.0 / period))
    sin_t, cos_t = sin_cos_turns(turn * (1.0 / period))
    waves = jnp.concatenate([cos_t, -sin_t])
    wave_high = waves.astype(BF16)
    wave_low = (waves - wave_high.astype(F32)).astype(BF16)
    wave_both = jnp.concatenate([wave_high, wave_low])
    dot = lambda a, b: jnp.dot(a, b, preferred_element_type=F32)
    core = lax.axis_index("gx") % 2
    for traces, half in ((trace_ref[0], core), (other_ref[0], 1 - core)):
        at = pl.ds(pl.multiple_of(half * 128, 128), 128)
        traces = traces * F32(scale)
        high = traces.astype(BF16)
        low = (traces - high.astype(F32)).astype(BF16)
        both = dot(wave_both, high)
        added = both[0 : 2 * bins] + (both[2 * bins :] + dot(wave_high, low))
        out_ref[0, :, at] = spec_ref[0, :, at] + added[0:bins]
        out_ref[1, :, at] = spec_ref[1, :, at] + added[bins:]


def swap(odd_even, even_odd, axis):
    count = lax.axis_size(axis)
    pairs = [(i, ((i + 1) ^ 1) - 1) for i in range(1, count) if ((i + 1) ^ 1) - 1 < count]
    got = lax.ppermute(odd_even, axis, pairs)
    return got, lax.ppermute(even_odd, axis, [(i, i ^ 1) for i in range(count) if i ^ 1 < count])


def body(pressure, previous, material, slot_cell, angles, spectra_in):
    tx, ty, nz = pressure.shape
    ngx, ngy = lax.axis_size("gx"), lax.axis_size("gy")
    shape = lambda *s: jax.ShapeDtypeStruct(s, F32)
    window = lambda kind: lambda *refs: window_kernel(kind, tx, ty, *refs)
    wide, thin = (3 * tx, ty + 2 * Y, nz), (3 * tx, ty + 2 * W, nz)
    scratch = lambda s: [pltpu.VMEM(s, F32)] * 2

    def count(tiles):
        return shape(len(tiles), 8, nz)

    cover = pl.CostEstimate(flops=3 * 10**10, transcendentals=0, bytes_accessed=1)

    def exchange_both(fields, state, y_b, y_a, x_b, x_a):
        y_rows = swap(y_b, y_a, "gy")
        ahead = swap(x_b, x_a, "gx")
        size = count(split_tiles(fields, tx, ty, 2 * W)[1])
        own, x_b, x_a = call(
            lambda *refs: join_kernel(fields, tx, ty, *refs), [shape(*state.shape[:1], *wide[1:]), size, size], name="join", cost=cover
        )(state, *y_rows)
        return [own, *ahead, *swap(x_b, x_a, "gx")]

    def exchange_x(own, *messages):
        return [own, *swap(*messages, "gx")]

    cells = jnp.concatenate([slot_cell, slot_cell])[None, :]
    tile = (tx, ty, nz)
    hbm = pl.BlockSpec(memory_space=pltpu.HBM)
    state = call(
        prepare_kernel,
        [shape(3 * tx, ty, nz)] + [shape(3 * tx, Y, nz)] * 2 + [count(split_tiles(3, tx, ty, 2 * W)[0])] * 2,
        [pltpu.VMEM(tile, F32), pltpu.VMEM(tile, F32), pltpu.VMEM(tile, jnp.int32), pltpu.SemaphoreType.DMA((3,))],
        name="prepare",
        specs=[hbm] * 3,
    )(*(pltpu.with_memory_space_constraint(v, pltpu.HBM) for v in (pressure, previous, material)))
    observers = angles.shape[1]
    half = jax.ShapeDtypeStruct((128, observers), BF16)
    high, low, token = call(lambda *refs: waves_kernel(tx, ty, nz, *refs), [half, half, shape(8, 128)], name="waves")(cells, angles)

    fields = shape(W, *tile)
    sample = lambda *v: call(sample_kernel, shape(len(v) * W, 128), name="sample")(cells, *v)
    message = count(message_tiles(2, tx, ty, W))
    between = [shape(2 * tx + 2, *thin[1:]), message, message, fields]
    *own, first, p, q, r = call(window("first"), between + [shape(*wide)] * 3, scratch(wide), name="window_first")(
        *exchange_both(3, *state), token
    )
    coefs = call(lambda *refs: narrow_kernel(ty, *refs), [shape(*thin)] * 3, name="narrow")(p, q, r)
    *state, second = call(
        window("inner"),
        [shape(2 * tx + 2, ty, nz)] + [shape(2 * tx, Y, nz)] * 2 + [count(split_tiles(2, tx, ty, 2 * W)[0])] * 2 + [fields],
        scratch(thin),
        name="window_inner",
    )(*exchange_x(*own), *coefs)
    early = sample(first, second)
    *own, third = call(window("wide"), between, scratch(wide), name="window_wide")(*exchange_both(2, *state), early, p, q, r)
    current, before, series = call(
        window("last"), [shape(*tile), shape(*tile), shape(STEPS, 128)], scratch(thin), name="window_last"
    )(*exchange_x(*own), cells, *coefs, early, sample(third))

    share = call(project_kernel, shape(2 * ngy, STEPS, 128), name="project")(series, high, low)
    rows = [list(range(k, k + 2 * ngy)) for k in range(0, ngx * ngy, 2 * ngy)]
    share = lax.all_to_all(share, ("gx", "gy"), 0, 0, tiled=True, axis_index_groups=rows)
    share = call(total_kernel, shape(ngx // 2, STEPS, 128), name="row_total")(share)
    chips = [list(range(core, ngx, 2)) for core in range(2)]
    share = lax.all_to_all(share, "gx", 0, 0, tiled=True, axis_index_groups=chips)
    traces = call(total_kernel, shape(1, STEPS, 128), name="total")(share)
    other = lax.ppermute(traces, "gx", [(i, i ^ 1) for i in range(ngx)])
    scale = float(slot_cell.shape[0] * ngx * ngy) ** -0.5
    bins = spectra_in.shape[1] * ngx
    spectra = call(lambda *refs: spectra_kernel(scale, bins, *refs), shape(*spectra_in.shape), name="spectra")(
        traces, other, spectra_in
    )
    return current, before, spectra


def solution(mesh):
    return jax.shard_map(
        body,
        mesh=mesh,
        in_specs=(
            P("gx", "gy", None),
            P("gx", "gy", None),
            P("gx", "gy", None),
            P(("gx", "gy")),
            P(),
            P(None, "gx", "gy"),
        ),
        out_specs=(P("gx", "gy", None), P("gx", "gy", None), P(None, "gx", "gy")),
        check_vma=False,
    )
```

```python
import jax
import jax.numpy as jnp
from jax import lax
from jax.experimental import pallas as pl
from jax.experimental.pallas import tpu as pltpu
from jax.sharding import PartitionSpec as P

STEPS = 16
START = 3000
KAPPA = 0.37
W = 4
Y = 8
F32 = jnp.float32
BF16 = jnp.bfloat16
TURN = 6.283185307179586


def call(kernel, outs, scratch=(), name=None, specs=None, cost=None, out_specs=None):
    more = {} if specs is None else {"in_specs": specs}
    if out_specs is not None:
        more["out_specs"] = out_specs
    return pl.pallas_call(
        kernel,
        out_shape=outs,
        scratch_shapes=list(scratch),
        compiler_params=pltpu.CompilerParams(vmem_limit_bytes=16 * 1024 * 1024),
        name=name,
        cost_estimate=cost,
        **more,
    )


def plane_sets(fields, tx):
    return [(0, tx), (tx + 1, 2 * tx + 1)] if fields == 2 else [(k * tx, (k + 1) * tx) for k in range(fields)]


def write_edges(state, b_ref, a_ref, fields, tx, ty):
    even = lax.axis_index("gy") % 2 == 0
    top, bottom = ty - Y, 0
    for ref, row in ((a_ref, jnp.where(even, top, bottom)), (b_ref, jnp.where(even, bottom, top))):
        for k, (lo, hi) in enumerate(plane_sets(fields, tx)):
            ref[k * tx : (k + 1) * tx] = state[lo:hi, pl.ds(pl.multiple_of(row, 8), Y)]


def openness(mat):
    return jnp.where(mat == 1, 0.0, jnp.where(mat == 2, F32(1.0) / F32(1.5), F32(1.0)))


def edges_kernel(cur_hbm, bef_hbm, mat_hbm, y_b, y_a, cur_ref, bef_ref, mat_ref, sems):
    tx, ty, _ = cur_hbm.shape
    even = lax.axis_index("gy") % 2 == 0
    top, bottom = ty - Y, 0
    copies = []
    for k, (src, dst) in enumerate(((mat_hbm, mat_ref), (cur_hbm, cur_ref), (bef_hbm, bef_ref))):
        for side, row in enumerate((jnp.where(even, bottom, top), jnp.where(even, top, bottom))):
            rows = pl.ds(pl.multiple_of(row, 8), Y)
            copies.append(pltpu.make_async_copy(src.at[:, rows], dst.at[side], sems.at[2 * k + side]))
    for copy in copies:
        copy.start()
    for copy in copies:
        copy.wait()
    for side, ref in enumerate((y_b, y_a)):
        mat = mat_ref[side]
        ref[0:tx] = jnp.where(mat == 1, 0.0, cur_ref[side])
        ref[tx : 2 * tx] = jnp.where(mat == 1, 0.0, bef_ref[side])
        ref[2 * tx :] = openness(mat)


def prepare_kernel(cur_hbm, bef_hbm, mat_hbm, state_ref, x_b, x_a, cur_ref, bef_ref, mat_ref, sems):
    tx, ty, _ = cur_ref.shape
    pairs = ((mat_hbm, mat_ref), (cur_hbm, cur_ref), (bef_hbm, bef_ref))
    copies = [pltpu.make_async_copy(src, dst, sems.at[k]) for k, (src, dst) in enumerate(pairs)]
    for copy in copies:
        copy.start()
    copies[0].wait()
    mat = mat_ref[...]
    state_ref[2 * tx :] = openness(mat)
    copies[1].wait()
    state_ref[0:tx] = jnp.where(mat == 1, 0.0, cur_ref[...])
    copies[2].wait()
    state_ref[tx : 2 * tx] = jnp.where(mat == 1, 0.0, bef_ref[...])
    write_messages(state_ref, x_b, x_a, split_tiles(3, tx, ty, 2 * W)[0], 3, tx, ty)


def message_tiles(fields, tx, ty, reach):
    tiles = []
    for field in range(fields):
        late = 1 if field == 1 else 0
        for d in range(1, W + 1 - late):
            known = fields == 2 and late and d == 1
            if not known:
                tiles += [(field, d, 8 * k, False) for k in range(ty // 8)]
            rows = reach - d - late
            if rows > 4:
                tiles += [(field, d, ty, False), (field, d, ty + 8, False)]
            elif rows > 0 and not known:
                tiles.append((field, d, ty, True))
    return tiles


def split_tiles(fields, tx, ty, reach):
    tiles = message_tiles(fields, tx, ty, reach)
    return [t for t in tiles if t[2] < ty], [t for t in tiles if t[2] >= ty]


def write_messages(own, b_ref, a_ref, tiles, fields, tx, ty):
    odd = lax.axis_index("gx") % 2
    wide = own.shape[1] == ty + 16
    low = lax.broadcasted_iota(jnp.int32, (8, own.shape[2]), 0) < 4
    for k, (field, d, row, packed) in enumerate(tiles):
        for ref, below in ((a_ref, odd), (b_ref, 1 - odd)):
            plane = plane_sets(fields, tx)[field][0] + below * (d - 1) + (1 - below) * (tx - d)
            tile = own[plane, row : row + 8]
            if packed and wide:
                tile = jnp.where(low, tile, own[plane, row + 8 : row + 16])
            ref[k] = tile


def read_messages(targets, b_ref, a_ref, tiles, tx, ty):
    odd = lax.axis_index("gx") % 2
    wide = targets[0].shape[1] == ty + 16
    for k, (field, d, row, packed) in enumerate(tiles):
        for ref, below in ((a_ref, odd), (b_ref, 1 - odd)):
            plane = below * (tx - d) + (1 - below) * (2 * tx + d - 1)
            tile = ref[k]
            targets[field][plane, row : row + 8] = tile
            if packed and wide:
                targets[field][plane, row + 8 : row + 16] = tile


def join_kernel(fields, tx, ty, state_ref, y_b, y_a, own_ref, odd_even_ref, even_odd_ref):
    odd = lax.axis_index("gy") % 2
    own_ref[:, 0:ty] = state_ref[...]
    for ref, row in ((y_a, ty + 8 * odd), (y_b, ty + 8 - 8 * odd)):
        for k, (lo, hi) in enumerate(plane_sets(fields, tx)):
            own_ref[lo:hi, pl.ds(pl.multiple_of(row, 8), 8)] = ref[k * tx : (k + 1) * tx]
    write_messages(own_ref, odd_even_ref, even_odd_ref, split_tiles(fields, tx, ty, 2 * W)[1], fields, tx, ty)


def around(plane, x):
    v = plane(x)
    lane = lax.broadcasted_iota(jnp.int32, (v.shape[0], 128), 1)
    parts = [v[:, k : k + 128] for k in range(0, v.shape[1], 128)]
    ahead = [pltpu.roll(p, 1, 1) for p in parts]
    back = [pltpu.roll(p, 127, 1) for p in parts]
    below = [jnp.where(lane == 0, a, b) for a, b in zip([0.0, *ahead[:-1]], ahead)]
    above = [jnp.where(lane == 127, a, b) for a, b in zip([*back[1:], 0.0], back)]
    z_sum = jnp.concatenate([a + b for a, b in zip(below, above)], axis=1)
    y_sum = pltpu.roll(v, 1, 0) + pltpu.roll(v, v.shape[0] - 1, 0)
    return v, (plane(x - 1) + plane(x + 1)) + (y_sum + z_sum)


def advance_step(cur, bef, coefs, lo, hi):
    rows = cur.shape[1] // 8
    row = lax.broadcasted_iota(jnp.int32, (8, 128), 0)
    lane = lax.broadcasted_iota(jnp.int32, (8, 128), 1)
    n = cur.shape[2] // 128
    for k in range(rows):
        before, after = (k - 1) % rows, (k + 1) % rows
        at = slice(8 * k, 8 * k + 8)
        load = lambda x, i, j: cur[x, 8 * i : 8 * i + 8, 128 * j : 128 * j + 128]
        line = lambda x: [load(x, k, j) for j in range(n)]
        down, here = line(lo - 1), line(lo)
        for x in range(lo, hi):
            up = line(x + 1)
            ahead = [pltpu.roll(p, 1, 1) for p in here]
            back = [pltpu.roll(p, 127, 1) for p in here]
            for j in range(n):
                cols = slice(128 * j, 128 * j + 128)
                z = jnp.where(lane == 0, ahead[j - 1] if j else 0.0, ahead[j])
                z = z + jnp.where(lane == 127, back[j + 1] if j + 1 < n else 0.0, back[j])
                y = pltpu.roll(jnp.where(row == 7, load(x, before, j), here[j]), 1, 0)
                y = y + pltpu.roll(jnp.where(row == 0, load(x, after, j), here[j]), 7, 0)
                total = (down[j] + up[j]) + (y + z)
                new = coefs[0][x, at, cols] * here[j] + coefs[1][x, at, cols] * total
                bef[x, at, cols] = new + coefs[2][x, at, cols] * bef[x, at, cols]
            down, here = here, up


def narrow(v, ty):
    above, below = v[..., ty : ty + 8, :], v[..., ty + 8 :, :]
    low = lax.broadcasted_iota(jnp.int32, above.shape, above.ndim - 2) < 4
    return jnp.concatenate([v[..., 0:ty, :], jnp.where(low, above, below)], axis=-2)


def sampler(cell, tx, ty, nz):
    safe = jnp.maximum(cell, 0)
    lane = lax.broadcasted_iota(jnp.int32, (1, 128), 1)
    z_of = safe % nz + (lane >= 64).astype(jnp.int32)
    row_of = jnp.where(cell >= 0, safe // nz, -1)
    zhot = (lax.broadcasted_iota(jnp.int32, (nz, 128), 0) == z_of).astype(BF16)
    rhot = lax.broadcasted_iota(jnp.int32, (tx * ty, 128), 0) == row_of

    def pick(field):
        now = field.reshape(tx * ty, nz)
        high = now.astype(BF16)
        low = (now - high.astype(F32)).astype(BF16)
        dot = lambda a: jnp.dot(a, zhot, preferred_element_type=F32)
        return jnp.sum(jnp.where(rhot, dot(high) + dot(low), 0.0), axis=0, keepdims=True)

    return pick


def sample_kernel(cell_ref, *refs):
    *rounds, out_ref = refs
    pick = sampler(cell_ref[...], *rounds[0].shape[1:])
    for k in range(len(rounds) * W):
        out_ref[pl.ds(k, 1), :] = pick(rounds[k // W][k % W])


def narrow_kernel(ty, *refs):
    for src, dst in zip(refs[:3], refs[3:]):
        dst[...] = narrow(src[...], ty)


def window_kernel(kind, tx, ty, *refs):
    refs = list(refs)
    take = lambda n: [refs.pop(0) for _ in range(n)]
    own, x_b, x_a = take(3)
    from_y = take(2) if kind in ("first", "wide") else ()
    (extra,) = take(1) if kind != "inner" else (None,)
    if kind != "first":
        coefs = take(3)
    done = take(2) if kind == "last" else ()
    if kind == "last":
        out_cur, out_bef, series_ref = take(3)
    else:
        state_ref, *rest = take(5 if kind == "inner" else 3)
        (fields_ref,) = take(1)
    if kind == "first":
        coefs = take(3)
        gain_ref = coefs[2]
    one, two = take(2)
    nz = own.shape[2]
    targets = [one, two] + ([gain_ref] if kind == "first" else [])
    if kind == "first":
        for field, target in enumerate(targets):
            target[tx : 2 * tx] = own[field * tx : (field + 1) * tx]
    else:
        one[tx : 2 * tx] = own[0:tx]
        two[tx - 1 : 2 * tx + 1] = own[tx:]
    if from_y:
        for pair, tiles in zip(((x_b, x_a), from_y), split_tiles(len(targets), tx, ty, 2 * W)):
            read_messages(targets, *pair, tiles, tx, ty)
    else:
        read_messages(targets, x_b, x_a, message_tiles(2, tx, ty, W), tx, ty)
    if kind == "first":
        for k in (0, 1):
            coefs[k][...] = jnp.zeros(coefs[k].shape, F32)
        opened = lambda i: jnp.where(gain_ref[i] > 0.0, F32(1.0), F32(0.0))
        for x in range(1, 3 * tx - 1):
            gain = gain_ref[x]
            coefs[0][x] = gain * (2.0 - 0.25 * around(opened, x)[1])
            coefs[1][x] = 0.25 * gain
        for x in range(3 * tx):
            gain_ref[x] = 1.0 - 2.0 * gain_ref[x]
    if kind == "last":
        pick = sampler(extra[...], tx, ty, nz)
    picks = []
    for step in range(1, W + 1):
        cur, bef = (one, two) if step % 2 else (two, one)
        advance_step(cur, bef, coefs, step, 3 * tx - step)
        if kind == "last":
            picks.append(pick(bef[tx : 2 * tx, 0:ty]))
        else:
            fields_ref[step - 1] = bef[tx : 2 * tx, 0:ty]
    cur, bef = (one, two) if W % 2 == 0 else (two, one)
    if kind == "last":
        out_cur[...] = cur[tx : 2 * tx, 0:ty]
        out_bef[...] = bef[tx : 2 * tx, 0:ty]
        series_ref[...] = jnp.concatenate([*(d[...] for d in done), *picks])
        return
    cut = (lambda v: v[:, 0:ty]) if kind == "inner" else (lambda v: narrow(v, ty))
    state_ref[0:tx] = cut(cur[tx : 2 * tx])
    state_ref[tx:] = cut(bef[tx - 1 : 2 * tx + 1])
    if kind == "inner":
        write_edges(state_ref, *rest[:2], 2, tx, ty)
        write_messages(state_ref, *rest[2:], split_tiles(2, tx, ty, 2 * W)[0], 2, tx, ty)
    else:
        write_messages(state_ref, *rest, message_tiles(2, tx, ty, W), 2, tx, ty)


def sin_cos_turns(p):
    r = p - jnp.floor(p + 0.5)
    q = r * r
    s = F32(-0.00702838626472677)
    for k in (0.0820504017189708, -0.599252197803835, 2.55016331894515, -5.16771276462447, 3.14159265353629):
        s = s * q + F32(k)
    s = s * r
    c = F32(-0.0243963243010939)
    for k in (0.234937313786045, -1.33521200304381, 4.0587091595557, -4.93480213707881, 0.999999999779904):
        c = c * q + F32(k)
    return 2.0 * s * c, 1.0 - 2.0 * s * s


def waves_kernel(tx, ty, nz, cell_ref, angle_ref, high_ref, low_ref, token_ref):
    token_ref[...] = jnp.zeros(token_ref.shape, F32)
    slots = cell_ref.shape[1] // 2
    cells = jnp.broadcast_to(cell_ref[...], (8, 2 * slots)).astype(F32)
    cells = jnp.concatenate([cells] * (2 * slots // 8)).T[0:slots, 0:1]
    cells = jnp.maximum(cells, 0.0).astype(jnp.int32)
    x_of = (lax.axis_index("gx") * tx + cells // (ty * nz)).astype(F32)
    y_of = (lax.axis_index("gy") * ty + cells // nz % ty).astype(F32)
    z_of = (cells % nz).astype(F32)
    width = 512
    for k in range(0, angle_ref.shape[1], width):
        cols = slice(k, k + width)
        sin_e, cos_e = sin_cos_turns(angle_ref[0:1, cols] * (1.0 / TURN))
        sin_a, cos_a = sin_cos_turns(angle_ref[1:2, cols] * (1.0 / TURN))
        ux, uy, uz = cos_e * cos_a, cos_e * sin_a, sin_e
        s, c = sin_cos_turns((KAPPA / TURN) * (ux * x_of + uy * y_of + uz * z_of))
        for half, v in enumerate((uz * s - c, c)):
            rows = slice(half * slots, (half + 1) * slots)
            high = v.astype(BF16)
            high_ref[rows, cols] = high
            low_ref[rows, cols] = (v - high.astype(F32)).astype(BF16)


def project_kernel(series_ref, high_ref, low_ref, out_ref):
    v = series_ref[...]
    high = v.astype(BF16)
    low = (v - high.astype(F32)).astype(BF16)
    dot = lambda a, b: jnp.dot(a, b, preferred_element_type=F32)
    both = dot(jnp.concatenate([high, low]), high_ref[...])
    total = (both[STEPS:] + dot(high, low_ref[...])) + both[0:STEPS]
    ngy = out_ref.shape[0] // 2
    for core in range(2):
        for j in range(ngy):
            at = (2 * j + core) * 128
            out_ref[core * ngy + j] = total[:, at : at + 128]


def total_kernel(part_ref, out_ref):
    total = jnp.sum(part_ref[...], axis=0)
    for k in range(out_ref.shape[0]):
        out_ref[k] = total


def spectra_kernel(scale, bin_total, trace_ref, other_ref, spec_ref, out_ref):
    bins = spec_ref.shape[1]
    period = 2 * (bin_total + 1)
    bin_of = lax.axis_index("gx") * bins + lax.broadcasted_iota(jnp.int32, (bins, STEPS), 0) + 1
    step_of = lax.broadcasted_iota(jnp.int32, (bins, STEPS), 1) + START
    turn = (step_of * bin_of).astype(F32)
    turn = turn - period * jnp.floor(turn * (1.0 / period))
    sin_t, cos_t = sin_cos_turns(turn * (1.0 / period))
    waves = jnp.concatenate([cos_t, -sin_t])
    wave_high = waves.astype(BF16)
    wave_low = (waves - wave_high.astype(F32)).astype(BF16)
    wave_both = jnp.concatenate([wave_high, wave_low])
    dot = lambda a, b: jnp.dot(a, b, preferred_element_type=F32)
    core = lax.axis_index("gx") % 2
    for traces, half in ((trace_ref[0], core), (other_ref[0], 1 - core)):
        at = pl.ds(pl.multiple_of(half * 128, 128), 128)
        traces = traces * F32(scale)
        high = traces.astype(BF16)
        low = (traces - high.astype(F32)).astype(BF16)
        both = dot(wave_both, high)
        added = both[0 : 2 * bins] + (both[2 * bins :] + dot(wave_high, low))
        out_ref[0, :, at] = spec_ref[0, :, at] + added[0:bins]
        out_ref[1, :, at] = spec_ref[1, :, at] + added[bins:]


def swap(odd_even, even_odd, axis):
    count = lax.axis_size(axis)
    pairs = [(i, ((i + 1) ^ 1) - 1) for i in range(1, count) if ((i + 1) ^ 1) - 1 < count]
    got = lax.ppermute(odd_even, axis, pairs)
    return got, lax.ppermute(even_odd, axis, [(i, i ^ 1) for i in range(count) if i ^ 1 < count])


def body(pressure, previous, material, slot_cell, angles, spectra_in):
    tx, ty, nz = pressure.shape
    ngx, ngy = lax.axis_size("gx"), lax.axis_size("gy")
    shape = lambda *s: jax.ShapeDtypeStruct(s, F32)
    window = lambda kind: lambda *refs: window_kernel(kind, tx, ty, *refs)
    wide, thin = (3 * tx, ty + 2 * Y, nz), (3 * tx, ty + 2 * W, nz)
    scratch = lambda s: [pltpu.VMEM(s, F32)] * 2

    def count(tiles):
        return shape(len(tiles), 8, nz)

    cover = pl.CostEstimate(flops=3 * 10**10, transcendentals=0, bytes_accessed=1)

    def exchange_both(fields, state, y_b, y_a, x_b, x_a):
        y_rows = swap(y_b, y_a, "gy")
        ahead = swap(x_b, x_a, "gx")
        size = count(split_tiles(fields, tx, ty, 2 * W)[1])
        own, x_b, x_a = call(
            lambda *refs: join_kernel(fields, tx, ty, *refs), [shape(*state.shape[:1], *wide[1:]), size, size], name="join", cost=cover
        )(state, *y_rows)
        return [own, *ahead, *swap(x_b, x_a, "gx")]

    def exchange_x(own, *messages):
        return [own, *swap(*messages, "gx")]

    cells = jnp.concatenate([slot_cell, slot_cell])[None, :]
    tile = (tx, ty, nz)
    hbm = pl.BlockSpec(memory_space=pltpu.HBM)
    args = [pltpu.with_memory_space_constraint(v, pltpu.HBM) for v in (pressure, previous, material)]
    edge = (2, tx, Y, nz)
    y_messages = call(
        edges_kernel,
        [shape(3 * tx, Y, nz)] * 2,
        [pltpu.VMEM(edge, F32), pltpu.VMEM(edge, F32), pltpu.VMEM(edge, jnp.int32), pltpu.SemaphoreType.DMA((6,))],
        name="edges",
        specs=[hbm] * 3,
    )(*args)
    state, *x_messages = call(
        prepare_kernel,
        [shape(3 * tx, ty, nz)] + [count(split_tiles(3, tx, ty, 2 * W)[0])] * 2,
        [pltpu.VMEM(tile, F32), pltpu.VMEM(tile, F32), pltpu.VMEM(tile, jnp.int32), pltpu.SemaphoreType.DMA((3,))],
        name="prepare",
        specs=[hbm] * 3,
    )(*args)
    state = [state, *y_messages, *x_messages]
    observers = angles.shape[1]
    half = jax.ShapeDtypeStruct((128, observers), BF16)
    high, low, token = call(lambda *refs: waves_kernel(tx, ty, nz, *refs), [half, half, shape(8, 128)], name="waves")(cells, angles)

    fields = shape(W, *tile)
    sample = lambda *v: call(sample_kernel, shape(len(v) * W, 128), name="sample")(cells, *v)
    message = count(message_tiles(2, tx, ty, W))
    between = [shape(2 * tx + 2, *thin[1:]), message, message, fields]
    *own, first, p, q, r = call(window("first"), between + [shape(*wide)] * 3, scratch(wide), name="window_first")(
        *exchange_both(3, *state), token
    )
    coefs = call(lambda *refs: narrow_kernel(ty, *refs), [shape(*thin)] * 3, name="narrow")(p, q, r)
    *state, second = call(
        window("inner"),
        [shape(2 * tx + 2, ty, nz)] + [shape(2 * tx, Y, nz)] * 2 + [count(split_tiles(2, tx, ty, 2 * W)[0])] * 2 + [fields],
        scratch(thin),
        name="window_inner",
    )(*exchange_x(*own), *coefs)
    early = sample(first, second)
    *own, third = call(window("wide"), between, scratch(wide), name="window_wide")(*exchange_both(2, *state), early, p, q, r)
    current, before, series = call(
        window("last"), [shape(*tile), shape(*tile), shape(STEPS, 128)], scratch(thin), name="window_last"
    )(*exchange_x(*own), cells, *coefs, early, sample(third))

    share = call(project_kernel, shape(2 * ngy, STEPS, 128), name="project")(series, high, low)
    rows = [list(range(k, k + 2 * ngy)) for k in range(0, ngx * ngy, 2 * ngy)]
    share = lax.all_to_all(share, ("gx", "gy"), 0, 0, tiled=True, axis_index_groups=rows)
    share = call(total_kernel, shape(ngx // 2, STEPS, 128), name="row_total")(share)
    chips = [list(range(core, ngx, 2)) for core in range(2)]
    share = lax.all_to_all(share, "gx", 0, 0, tiled=True, axis_index_groups=chips)
    traces = call(total_kernel, shape(1, STEPS, 128), name="total")(share)
    other = lax.ppermute(traces, "gx", [(i, i ^ 1) for i in range(ngx)])
    scale = float(slot_cell.shape[0] * ngx * ngy) ** -0.5
    bins = spectra_in.shape[1] * ngx
    spectra = call(lambda *refs: spectra_kernel(scale, bins, *refs), shape(*spectra_in.shape), name="spectra")(
        traces, other, spectra_in
    )
    return current, before, spectra


def solution(mesh):
    return jax.shard_map(
        body,
        mesh=mesh,
        in_specs=(
            P("gx", "gy", None),
            P("gx", "gy", None),
            P("gx", "gy", None),
            P(("gx", "gy")),
            P(),
            P(None, "gx", "gy"),
        ),
        out_specs=(P("gx", "gy", None), P("gx", "gy", None), P(None, "gx", "gy")),
        check_vma=False,
    )
```
